32 devices in a mesh: user: 8 (over z, y), item: 4 (over x, core).
Axes of the slice: x: 2, y: 2, z: 4, core: 2. Of those that a mesh axis runs over, the one named last changes fastest.
Arguments:
- v_start: bfloat16 [32768, 64], P(('user', 'item')), may hold values from -6 to 6
- locked: bfloat16 [32768, 32], P(('user', 'item')), may hold values from -0.0625 to 0.0625
- tile_rows: int32 [32, 512], P(('user', 'item')), may hold values from 0 to 63, as said below
- tile_cols: int32 [32, 512], P(('user', 'item')), may hold values from 0 to 63
- tile_seeds: int32 [32, 512], P(('user', 'item')), may hold values from 0 to 1048575
- tile_count: int32 [32, 1], P(('user', 'item')), may hold values from 128 to 512, as said below
Outputs:
- u_factor: bfloat16 [65536, 64], P(('user', 'item'))
- v_next: float32 [32768, 64], P(('user', 'item'))
The draws below stay inside these ranges and needn't reach their ends.
Inputs may be any that keep to these rules, and one draw needn't show every extreme that they name: `tile_count`: at most 512 live slots a device, and one device holds exactly 512. `tile_rows`: A device's slots name distinct (row, column) pairs.
All inputs are finite; a program needn't handle non-finite values.
Results may differ from the reference program's by a relative error of at most 0.0049.
Values may be sent and summed in bfloat16 or wider, within the bound.
A program may use at most 64 MiB of HBM per device.

```python
import jax
import jax.numpy as jnp
from jax import lax

TILE = 128
K = 64
LOCK = 32
RB = 64
CAP = 512
CB = 64
SHARD = 1024
USERS = 65536
ITEMS = 32768
N_USER = 8
N_ITEM = 4


def slot_positions(key):
    keys = jax.random.split(jax.random.fold_in(key, 7), N_USER * N_ITEM)
    return jax.vmap(lambda k: jax.random.permutation(k, RB * CB)[:CAP])(keys).astype(jnp.int32)


def draw_tile_rows(key, part):
    return slot_positions(key) // CB


def draw_tile_cols(key, part):
    return slot_positions(key) % CB


def draw_tile_seeds(key, part):
    return jax.random.randint(jax.random.fold_in(key, 17), (N_USER * N_ITEM, CAP), 0, 1048576, dtype=jnp.int32)


def draw_tile_count(key, part):
    total = N_USER * N_ITEM
    counts = jax.random.randint(jax.random.fold_in(key, 11), (total,), CAP // 4, CAP // 2 + 1, dtype=jnp.int32)
    busiest = jax.random.randint(jax.random.fold_in(key, 13), (), 0, total, dtype=jnp.int32)
    counts = jnp.where(jnp.arange(total, dtype=jnp.int32) == busiest, CAP, counts)
    return counts.reshape(total, 1)


def block_levels(stream_key, shape, pieces, least, top_value):
    factor_of = 1.0
    for axis_at, shards_of in pieces:
        heights = jax.random.uniform(jax.random.fold_in(jax.random.fold_in(stream_key, 6), axis_at), (shards_of,), jnp.float32, least / len(pieces), top_value / len(pieces))
        factor_of = factor_of * jnp.repeat(jnp.exp(heights), shape[axis_at] // shards_of).reshape((-1,) + (1,) * (len(shape) - 1 - axis_at))
    return factor_of


def normal_values(stream_key, extent, deviation, bound, cuts=(), kind=jnp.bfloat16):
    array = jax.random.normal(stream_key, extent, jnp.float32) * deviation
    if len(cuts) > 0:
        array = block_levels(stream_key, extent, cuts, -0.22, 0.18) * array
    return jnp.clip(array, min=-bound, max=bound).astype(kind)


def setup_inputs(seed: int = 0) -> dict:
    key_list = jax.random.split(jax.random.key(seed), 7)
    return {
        "v_start": normal_values(key_list[0], (ITEMS, K), 1.0, 6.0, ((0, 32),)),
        "locked": normal_values(key_list[1], (ITEMS, LOCK), (ITEMS // 4) ** -0.5, 0.0625, ((0, 32),)),
        "tile_rows": draw_tile_rows(jax.random.fold_in(key_list[6], 71), 0),
        "tile_cols": draw_tile_cols(jax.random.fold_in(key_list[6], 71), 0),
        "tile_seeds": draw_tile_seeds(jax.random.fold_in(key_list[6], 71), 0),
        "tile_count": draw_tile_count(jax.random.fold_in(key_list[6], 71), 0),
    }


tile_batch = 16

def tile_values(seeds):
    rowpos = lax.broadcasted_iota(jnp.int32, (TILE, TILE), 0)
    colpos = lax.broadcasted_iota(jnp.int32, (TILE, TILE), 1)
    hashed = (rowpos * TILE + colpos)[None, :, :] * 40503 + seeds[:, None, None] * 9973
    hashed = jnp.bitwise_xor(hashed, jnp.right_shift(hashed, 13))
    hashed = hashed * 1597334677
    hashed = jnp.bitwise_xor(hashed, jnp.right_shift(hashed, 16))
    levels = jnp.bitwise_and(jnp.right_shift(hashed, 8), 255) - 128
    return (levels.astype(jnp.float32) * (1.0 / 1024.0)).astype(jnp.bfloat16)

def group_slice(rows, cols, seeds, count, start):
    grows = lax.dynamic_slice_in_dim(rows, start, tile_batch)
    gcols = lax.dynamic_slice_in_dim(cols, start, tile_batch)
    gseeds = lax.dynamic_slice_in_dim(seeds, start, tile_batch)
    valid = start + jnp.arange(tile_batch, dtype=jnp.int32) < count
    return (grows, gcols, gseeds, valid)

def forward_pass(rows, cols, seeds, count, vblocks):

    def step(g, upart):
        grows, gcols, gseeds, valid = group_slice(rows, cols, seeds, count, g * tile_batch)
        tiles = tile_values(gseeds).astype(jnp.float32)
        prod = jnp.einsum('gab,gbk->gak', tiles, vblocks[gcols].astype(jnp.float32), precision=lax.Precision.HIGHEST)
        prod = jnp.where(valid[:, None, None], prod, 0.0)
        return upart.at[grows].add(prod)
    steps = (count + tile_batch - 1) // tile_batch
    return lax.fori_loop(0, steps, step, jnp.zeros((RB, TILE, K), jnp.float32))

def backward_pass(rows, cols, seeds, count, ublocks):

    def step(g, wpart):
        grows, gcols, gseeds, valid = group_slice(rows, cols, seeds, count, g * tile_batch)
        tiles = tile_values(gseeds).astype(jnp.float32)
        prod = jnp.einsum('gab,gak->gbk', tiles, ublocks[grows].astype(jnp.float32), precision=lax.Precision.HIGHEST)
        prod = jnp.where(valid[:, None, None], prod, 0.0)
        return wpart.at[gcols].add(prod)
    steps = (count + tile_batch - 1) // tile_batch
    return lax.fori_loop(0, steps, step, jnp.zeros((CB, TILE, K), jnp.float32))

def reference(v_start, locked, tile_rows, tile_cols, tile_seeds, tile_count):
    high = lax.Precision.HIGHEST
    lockf = locked.astype(jnp.float32)
    proj = jnp.dot(locked.T, v_start, preferred_element_type=jnp.float32)
    deflated = (v_start.astype(jnp.float32) - jnp.dot(lockf, proj, precision=high)).astype(jnp.bfloat16)
    dshards = deflated.reshape(N_USER, N_ITEM, SHARD, K)
    devices = jnp.arange(N_USER * N_ITEM, dtype=jnp.int32)

    def forward_dev(uacc, dev):
        uidx = dev // N_ITEM
        iidx = dev % N_ITEM
        vblocks = lax.dynamic_index_in_dim(dshards, iidx, 1, keepdims=False).reshape(CB, TILE, K)
        part = forward_pass(tile_rows[dev], tile_cols[dev], tile_seeds[dev], tile_count[dev, 0], vblocks)
        current = lax.dynamic_index_in_dim(uacc, uidx, 0, keepdims=False)
        return (lax.dynamic_update_index_in_dim(uacc, current + part, uidx, 0), None)
    uacc, _ = lax.scan(forward_dev, jnp.zeros((N_USER, RB, TILE, K), jnp.float32), devices)
    ublocks_all = uacc.astype(jnp.bfloat16)
    u_factor = ublocks_all.reshape(USERS, K)

    def backward_dev(wacc, dev):
        uidx = dev // N_ITEM
        iidx = dev % N_ITEM
        ublocks = lax.dynamic_index_in_dim(ublocks_all, uidx, 0, keepdims=False)
        part = backward_pass(tile_rows[dev], tile_cols[dev], tile_seeds[dev], tile_count[dev, 0], ublocks)
        return (wacc.at[iidx].add(part.reshape(CB * TILE, K)), None)
    wacc, _ = lax.scan(backward_dev, jnp.zeros((N_ITEM, CB * TILE, K), jnp.float32), devices)
    back = wacc.reshape(N_ITEM, N_USER, SHARD, K).transpose(1, 0, 2, 3).reshape(ITEMS, K)
    proj2 = jnp.dot(lockf.T, back, precision=high)
    rest = back - jnp.dot(lockf, proj2, precision=high)
    colsq = lax.optimization_barrier(jnp.sum(rest * rest, axis=0))
    v_next = rest / jnp.sqrt(colsq / ITEMS + 1e-06)
    return (u_factor, v_next)
```

```python
import functools

import jax
import jax.numpy as jnp
from jax import lax
from jax.experimental import pallas as pl
from jax.experimental.pallas import tpu as pltpu
from jax.sharding import PartitionSpec as P

TILE = 128
RB = 64
LIMIT = 16 << 20
BIG_LIMIT = 56 << 20
GROUP = 16
SPAN = 32
SCALE = 1.0 / 1024.0
HIGH = lax.Precision.HIGHEST
NT = (((1,), (1,)), ((), ()))
NN = (((1,), (0,)), ((), ()))


def fill(seeds, tiles_ref, first, last, flip):
    a = lax.broadcasted_iota(jnp.int32, (TILE, TILE), 0)
    b = lax.broadcasted_iota(jnp.int32, (TILE, TILE), 1)
    base = (b * TILE + a if flip else a * TILE + b) * 40503

    def step(g, carry):
        for j in range(GROUP):
            s = g * GROUP + j
            h = base + seeds[0, s] * 9973
            h = h ^ (h >> 13)
            h = h * 1597334677
            h = h ^ (h >> 16)
            levels = ((h >> 8) & 255) - 128
            tiles_ref[s] = levels.astype(jnp.float32).astype(jnp.bfloat16)
        return carry

    lax.fori_loop(first, last, step, 0)


def fill_kernel(flip, seeds, tiles_ref):
    fill(seeds, tiles_ref, 0, tiles_ref.shape[0] // GROUP, flip)


def product_kernel(forward, places, count, x_ref, tiles_ref, out_ref, acc):
    blocks = out_ref.shape[0]
    live = count[0, 0]
    acc[...] = jnp.zeros_like(acc)

    def step(g, carry):
        for j in range(SPAN):
            s = g * SPAN + j
            row, col = places[0, s] >> 16, places[0, s] & 65535
            source, target = (col, row) if forward else (row, col)
            target = jnp.where(s < live, target, blocks)
            acc[target] += lax.dot_general(
                x_ref[source], tiles_ref[s], NN, preferred_element_type=jnp.float32
            )
        return carry

    lax.fori_loop(0, lax.div(live + (SPAN - 1), SPAN), step, 0)
    out_ref[...] = (acc[:blocks] * SCALE).astype(out_ref.dtype)


VMEM_SPEC = pl.BlockSpec(memory_space=pltpu.VMEM)
SMEM_SPEC = pl.BlockSpec(memory_space=pltpu.SMEM)


def product(forward, places, count, x, tiles, nblocks, dtype):
    width, tile = x.shape[1:]
    return pl.pallas_call(
        functools.partial(product_kernel, forward),
        name="forward" if forward else "backward",
        out_shape=jax.ShapeDtypeStruct((nblocks, width, tile), dtype),
        in_specs=[SMEM_SPEC, SMEM_SPEC, VMEM_SPEC, VMEM_SPEC],
        out_specs=VMEM_SPEC,
        scratch_shapes=[pltpu.VMEM((nblocks + 1, width, tile), jnp.float32)],
        compiler_params=pltpu.CompilerParams(vmem_limit_bytes=LIMIT),
    )(places, count, x, tiles)


def blocks_of(x):
    return x.reshape(-1, TILE, x.shape[1]).transpose(0, 2, 1)


def rows_of(blocks):
    return blocks.transpose(0, 2, 1).reshape(-1, blocks.shape[1])


MESH = pl.DeviceIdType.MESH


def place():
    user = lax.axis_index("user")
    return lax.div(user, 2), lax.rem(user, 2), lax.axis_index("item")


def plane():
    z, y, item = place()
    n = 2 * lax.axis_size("item")
    me = y * lax.axis_size("item") + item
    out = []
    for o in range(1, n):
        p = lax.rem(me + o, n)
        out.append({"user": 2 * z + lax.div(p, n // 2), "item": lax.rem(p, n // 2)})
    return n, me, out


def column():
    z, y, item = place()
    n = lax.axis_size("user") // 2
    return n, z, [{"user": 2 * lax.rem(z + o, n) + y, "item": item} for o in range(1, n)]


def remote(src, dst, send, recv, device):
    return pltpu.make_async_remote_copy(
        src_ref=src, dst_ref=dst, send_sem=send, recv_sem=recv, device_id=device,
        device_id_type=MESH,
    )


def sems(*shape):
    return pltpu.SemaphoreType.DMA(shape)


def pack(tile_rows, tile_cols):
    return tile_rows * 65536 + tile_cols


HALVES = 2
PARTS = 4
WIDE_GROUP = 64


def split3(x):
    high = x.astype(jnp.bfloat16)
    rest = x - high.astype(jnp.float32)
    mid = rest.astype(jnp.bfloat16)
    low = (rest - mid.astype(jnp.float32)).astype(jnp.bfloat16)
    return high, mid, low


def f32(x):
    return x.astype(jnp.float32)


def start_sum(group, value, slots, send, recv):
    n, me, devices = group
    slots[me] = value
    copies = [
        remote(slots.at[me], slots.at[me], send.at[o], recv.at[o], device)
        for o, device in enumerate(devices)
    ]
    for copy in copies:
        copy.start()
    return copies


def end_sum(group, copies, slots):
    for copy in copies:
        copy.wait()
    total = slots[0]
    for i in range(1, group[0]):
        total = total + slots[i]
    return total


def round_kernel(
    items, count, rows_hbm, cols_hbm, seeds_hbm, v_hbm, lock_hbm, u_out, v_out,
    rows, cols, seeds, links, row_lanes, col_lanes, link_lanes, v_ref, lock3,
    tiles, flipped, sums, v0, v1, part0, part1, near, pair, far_part, u0, u1, w0, w1,
    inbox, outbox, back, slots_p, slots_c, last_p, last_c,
    in_sem, ag_s, ag_r, x_s, x_r, rs_s, rs_r, sp, rp, sc, rc, sp2, rp2, sc2, rc2,
):
    vbuf, part, ubuf, wbuf = (v0, v1), (part0, part1), (u0, u1), (w0, w1)
    nslots = tiles.shape[0]
    nlock = lock_hbm.shape[0]
    width = v_hbm.shape[0]
    wide = width // HALVES
    own = v_hbm.shape[1] // TILE
    cut = own // 2
    nblocks = v0.shape[0]
    z, y, item = place()
    side = lax.rem(item, 2)
    upper = lax.div(z, 2)
    mate = z + 1 - 2 * lax.rem(z, 2)
    adj, far = 2 - upper, 3 - 3 * upper
    mid = 1 - lax.div(lax.rem(z + 2, 3), 2)
    user = 2 * z + y

    def at(zz, yy):
        return {"user": 2 * zz + yy, "item": item}

    facing_dev, mate_dev, adj_dev, far_dev = at(z, 1 - y), at(mate, y), at(adj, y), at(far, y)
    sibling = {"user": user, "item": item + 1 - 2 * side}
    across = {"user": user, "item": lax.rem(item + 2, 4)}

    loads = [
        pltpu.make_async_copy(src, dst, in_sem.at[i])
        for i, (src, dst) in enumerate(
            (
                (v_hbm, v_ref),
                (lock_hbm, lock3.at[pl.ds(0, nlock)]),
                (rows_hbm, row_lanes),
                (cols_hbm, col_lanes),
                (rows_hbm, rows),
                (cols_hbm, cols),
                (seeds_hbm, seeds),
            )
        )
    ]
    for load in loads:
        load.start()
    barrier = pltpu.get_barrier_semaphore()
    peers = plane()[2] + column()[2]
    for device in peers:
        pl.semaphore_signal(barrier, inc=1, device_id=device, device_id_type=MESH)
    sums[nslots] = jnp.zeros((wide, TILE), jnp.float32)
    for load in loads:
        load.wait()
    lock = lock3[:nlock]
    lock3[nlock : 2 * nlock] = lock
    lock3[2 * nlock : 3 * nlock] = lock
    proj = lax.dot_general(lock, v_ref[...], NT, preferred_element_type=jnp.float32)
    gram = lax.dot_general(lock, lock, NT, preferred_element_type=jnp.float32)
    half = nlock // 2
    quarter = nlock // 4
    stats = jnp.concatenate(
        [
            jnp.concatenate([proj[:half], proj[half:]], axis=1),
            jnp.concatenate([gram[i * quarter : (i + 1) * quarter] for i in range(4)], axis=1),
        ],
        axis=0,
    )
    pl.semaphore_wait(barrier, len(peers))
    pending = start_sum(plane(), stats, slots_p, sp, rp)

    live = count[0, 0]
    slot_lane = lax.broadcasted_iota(jnp.int32, (TILE, nslots), 1)
    slot_row = lax.broadcasted_iota(jnp.int32, (TILE, nslots), 0)
    block_lane = lax.broadcasted_iota(jnp.int32, (TILE, TILE), 1)
    block_row = lax.broadcasted_iota(jnp.int32, (TILE, TILE), 0)
    for which, lanes in enumerate((row_lanes, col_lanes)):
        wide_lanes = jnp.broadcast_to(lanes[...], (TILE, nslots))
        previous = jnp.full((1, nslots), -1, jnp.int32)
        latest = jnp.full((1, TILE), -1, jnp.int32)
        for j in range(nslots // TILE):
            down = wide_lanes[:, j * TILE : (j + 1) * TILE].T
            here = slot_row + j * TILE
            hit = (jnp.tile(down, (1, nslots // TILE)) == wide_lanes) & (here < slot_lane)
            hit = jnp.where(hit & (here < live), here, -1)
            previous = jnp.maximum(previous, jnp.max(hit, axis=0, keepdims=True))
            here = block_row + j * TILE
            hit = jnp.where((down == block_lane) & (here < live), here, -1)
            latest = jnp.maximum(latest, jnp.max(hit, axis=0, keepdims=True))
        link_lanes[which : which + 1, :] = jnp.where(previous < 0, nslots, previous)
        link_lanes[2 + which : 3 + which, :TILE] = jnp.where(latest < 0, nslots, latest)
    place_links = pltpu.make_async_copy(link_lanes, links, in_sem.at[len(loads)])
    place_links.start()

    iota_a = lax.broadcasted_iota(jnp.int32, (TILE, TILE), 0)
    iota_b = lax.broadcasted_iota(jnp.int32, (TILE, TILE), 1)
    base = (iota_a * TILE + iota_b) * 40503

    def fill_some(first, last):
        def step(g, carry):
            for j in range(GROUP):
                s = g * GROUP + j
                h = base + seeds[0, s] * 9973
                h = h ^ (h >> 13)
                h = h * 1597334677
                h = h ^ (h >> 16)
                levels = (((h >> 8) & 255) - 128).astype(jnp.float32).astype(jnp.bfloat16)
                tiles[s] = levels
                flipped[s] = levels.T
            return carry

        lax.fori_loop(first, last, step, 0)

    groups = nslots // GROUP
    marks = [groups * i // 16 for i in (0, 2, 5, 8, 11, 14, 16)]
    fill_some(marks[0], marks[1])
    stats = end_sum(plane(), pending, slots_p)
    pending = start_sum(column(), stats, slots_c, sc, rc)
    fill_some(marks[1], marks[2])
    stats = end_sum(column(), pending, slots_c)
    gram = jnp.concatenate(
        [stats[half : half + quarter, i * nlock : (i + 1) * nlock] for i in range(4)], axis=0
    )
    proj = jnp.concatenate([stats[:half, :width], stats[:half, width:]], axis=0)
    projt = jnp.concatenate([proj, jnp.zeros_like(proj)], axis=1).T[:width]
    gone = jnp.dot(
        jnp.concatenate(split3(projt), axis=1), lock3[...], preferred_element_type=jnp.float32
    )
    deflated = (f32(v_ref[...]) - gone).astype(jnp.bfloat16)
    for h in range(HALVES):
        for j in range(own):
            vbuf[h][user * own + j] = deflated[h * wide : (h + 1) * wide, j * TILE : (j + 1) * TILE]

    def spread(h, zz, yy, si, ri, device, first=0, size=own):
        ref = vbuf[h].at[pl.ds((2 * zz + yy) * own + first, size)]
        return remote(ref, ref, ag_s.at[h, si], ag_r.at[h, ri], device)

    gather = []
    for h in range(HALVES):
        gather.append(
            dict(
                face=spread(h, z, y, 0, 0, facing_dev),
                cross=spread(h, z, y, 1, 2 - mid, adj_dev),
                mate=spread(h, z, y, 3, 3, mate_dev),
                dmate=spread(h, mate, y, 4, 4, facing_dev, 0, cut),
                dadj=spread(h, adj, y, 5, 5, facing_dev),
                dfar=spread(h, far, y, 6, 6, facing_dev),
                extra=spread(h, z, 1 - y, 7, 7, mate_dev, cut, own - cut),
                cadj=spread(h, adj, y, 8, 1, mate_dev),
                cfar=spread(h, far, y, 9, 2, mate_dev),
            )
        )

    def own_out(h):
        for name in ("face", "cross", "mate"):
            gather[h][name].start()

    def near_in(h):
        gather[h]["face"].wait_recv()
        gather[h]["extra"].start()
        gather[h]["mate"].wait_recv()
        gather[h]["dmate"].start()

    def beyond_in(h, name):
        gather[h]["c" + name].wait_recv()

        @pl.when(mid == 1)
        def _():
            gather[h]["c" + name].start()

        gather[h]["d" + name].start()

    def rest_in(h):
        for name in ("extra", "dmate", "dadj", "dfar"):
            gather[h][name].wait_recv()

    def all_sent(h):
        for name in ("face", "cross", "mate", "dmate", "dadj", "dfar", "extra"):
            gather[h][name].wait_send()

        @pl.when(mid == 1)
        def _():
            gather[h]["cadj"].wait_send()
            gather[h]["cfar"].wait_send()

    own_out(0)
    fill_some(marks[2], marks[3])
    near_in(0)
    own_out(1)
    fill_some(marks[3], marks[4])
    beyond_in(0, "adj")
    beyond_in(0, "far")
    fill_some(marks[4], marks[5])
    place_links.wait()
    near_in(1)
    fill_some(marks[5], marks[6])
    rest_in(0)

    def sweep(x, blocks, weights, which, first, last):
        zero = jnp.zeros((wide, TILE), jnp.bfloat16)

        def step(g, carry):
            for j in range(WIDE_GROUP // 2):
                s = g * WIDE_GROUP + 2 * j
                x0 = jnp.concatenate([x[blocks[0, s]], zero], axis=1)
                x1 = jnp.concatenate([zero, x[blocks[0, s + 1]]], axis=1)
                both = lax.dot_general(
                    jnp.concatenate([x0, x1], axis=0),
                    weights[pl.ds(s, 2)].reshape(2 * TILE, TILE),
                    NN,
                    preferred_element_type=jnp.float32,
                )
                sums[s] = sums[links[which, s]] + both[:wide]
                sums[s + 1] = sums[links[which, s + 1]] + both[wide:]
            return carry

        lax.fori_loop(first, last, step, 0)

    def collect(which, out, first, size):
        def step(g, carry):
            for j in range(8):
                r = first + g * 8 + j
                out[r] = (sums[links[2 + which, r]] * SCALE).astype(out.dtype)
            return carry

        lax.fori_loop(0, size // 8, step, 0)

    steps = nslots // WIDE_GROUP
    hop = RB // 2
    size = hop // PARTS

    def exchange(h, k):
        def one(i, src, src_at, dst, dst_at, device):
            return remote(
                src.at[pl.ds(src_at + k * size, size)],
                dst.at[pl.ds(dst_at + k * size, size)],
                x_s.at[h, i, k],
                x_r.at[h, i, k],
                device,
            )

        return (
            one(0, part[h], (1 - side) * hop, near.at[h], 0, sibling),
            one(1, pair.at[h], 0, far_part.at[h], 0, across),
            one(2, ubuf[h], side * hop, ubuf[h], side * hop, sibling),
        )

    def give(h):
        collect(0, part[h], (1 - side) * hop, hop)
        for k in range(PARTS):
            exchange(h, k)[0].start()
        collect(0, part[h], side * hop, hop)

    def swap(h, k):
        given, swapped, _ = exchange(h, k)
        given.wait_recv()
        mine = part[h][pl.ds(side * hop + k * size, size)]
        span = pl.ds(k * size, size)
        pair[h, span] = (f32(mine) + f32(near[h, span])).astype(pair.dtype)
        swapped.start()

    def settle(h, k):
        _, swapped, backward = exchange(h, k)
        swapped.wait_recv()
        span = pl.ds(k * size, size)
        total = f32(pair[h, span]) + f32(far_part[h, span])
        ubuf[h][pl.ds(side * hop + k * size, size)] = total.astype(jnp.bfloat16)
        backward.start()

    def settled(h):
        for k in range(PARTS):
            exchange(h, k)[2].wait_recv()

    def exchanged(h):
        for k in range(PARTS):
            for copy in exchange(h, k):
                copy.wait_send()

    per = RB // 4

    def write_u(h):
        for j in range(per):
            u_out[h * wide : (h + 1) * wide, j * TILE : (j + 1) * TILE] = ubuf[h][item * per + j]

    sweep(v0, cols, flipped, 0, 0, steps // 4)
    beyond_in(1, "adj")
    sweep(v0, cols, flipped, 0, steps // 4, steps // 2)
    beyond_in(1, "far")
    sweep(v0, cols, flipped, 0, steps // 2, steps)
    give(0)
    rest_in(1)

    def first_swaps(k, carry):
        sweep(v1, cols, flipped, 0, k * (steps // 8), (k + 1) * (steps // 8))
        swap(0, k)
        return carry

    lax.fori_loop(0, PARTS, first_swaps, 0)
    sweep(v1, cols, flipped, 0, PARTS * (steps // 8), steps)
    give(1)

    def second_swaps(k, carry):
        swap(1, k)
        settle(0, k)
        return carry

    lax.fori_loop(0, PARTS, second_swaps, 0)
    settled(0)

    def third(k, carry):
        sweep(u0, rows, tiles, 1, k * (steps // PARTS), (k + 1) * (steps // PARTS))
        settle(1, k)
        return carry

    lax.fori_loop(0, PARTS, third, 0)

    def piece(h, zz, yy, first=0, count=own):
        return wbuf[h].at[pl.ds((2 * zz + yy) * own + first, count)]

    def post(h, src, place_at, count, si, ri, device):
        return remote(
            src, inbox.at[h, pl.ds(place_at, count)], rs_s.at[h, si], rs_r.at[h, ri], device
        )

    box = dict(dmate=0, extra=cut, dadj=own, dfar=2 * own, cadj=3 * own, cfar=4 * own)
    box.update(mate=5 * own, cross=6 * own, face=7 * own)

    def stage(h, i):
        return outbox.at[h, pl.ds(i * own, own)]

    scatter = []
    for h in range(HALVES):
        scatter.append(
            dict(
                dfar=post(h, piece(h, far, 1 - y), box["dfar"], own, 0, 0, facing_dev),
                dadj=post(h, piece(h, adj, 1 - y), box["dadj"], own, 1, 1, facing_dev),
                extra=post(
                    h, piece(h, mate, 1 - y, cut, own - cut), box["extra"], own - cut, 2, 2, mate_dev
                ),
                dmate=post(h, piece(h, mate, 1 - y, 0, cut), box["dmate"], cut, 3, 3, facing_dev),
                cadj=post(h, stage(h, 0), box["cadj"], own, 4, 4, mate_dev),
                cfar=post(h, stage(h, 1), box["cfar"], own, 5, 5, mate_dev),
                xadj=post(h, stage(h, 0), box["cross"], own, 6, 6, adj_dev),
                xfar=post(h, stage(h, 1), box["cross"], own, 7, 6, far_dev),
                face=post(h, stage(h, 2), box["face"], own, 8, 8, facing_dev),
                mate=post(h, stage(h, 3), box["mate"], own, 9, 9, mate_dev),
            )
        )

    def scatter_first(h):
        for name in ("dfar", "dadj", "extra", "dmate"):
            scatter[h][name].start()

    def got(h, name, count=own):
        return f32(inbox[h, box[name] : box[name] + count])

    def block(h, zz, yy, first=0, count=own):
        return f32(wbuf[h][pl.ds((2 * zz + yy) * own + first, count)])

    def beyond_out(h, name, zz, i):
        scatter[h]["d" + name].wait_recv()

        @pl.when(mid == 0)
        def _():
            both = block(h, zz, y) + got(h, "d" + name)
            outbox[h, i * own : (i + 1) * own] = both.astype(outbox.dtype)
            scatter[h]["c" + name].start()

    def beyond_pass(h, name, zz, i):
        @pl.when(mid == 1)
        def _():
            scatter[h]["c" + name].wait_recv()
            both = block(h, zz, y) + got(h, "d" + name) + got(h, "c" + name)
            outbox[h, i * own : (i + 1) * own] = both.astype(outbox.dtype)
            scatter[h]["x" + name].start()

    def near_out(h):
        scatter[h]["extra"].wait_recv()
        outbox[h, 2 * own : 2 * own + cut] = wbuf[h][pl.ds((2 * z + 1 - y) * own, cut)]
        tail = block(h, z, 1 - y, cut, own - cut) + got(h, "extra", own - cut)
        outbox[h, 2 * own + cut : 3 * own] = tail.astype(outbox.dtype)
        scatter[h]["face"].start()
        scatter[h]["dmate"].wait_recv()
        head = block(h, mate, y, 0, cut) + got(h, "dmate", cut)
        outbox[h, 3 * own : 3 * own + cut] = head.astype(outbox.dtype)
        outbox[h, 3 * own + cut : 4 * own] = wbuf[h][pl.ds((2 * mate + y) * own + cut, own - cut)]
        scatter[h]["mate"].start()

    def total(h):
        scatter[h]["mate"].wait_recv()
        scatter[h]["face"].wait_recv()
        scatter[h]["xadj"].wait_recv()
        whole = block(h, z, y) + got(h, "mate") + got(h, "face") + got(h, "cross")
        for j in range(own):
            back[h * wide : (h + 1) * wide, j * TILE : (j + 1) * TILE] = whole[j]
        square = whole[0] * whole[0]
        for j in range(1, own):
            square = square + whole[j] * whole[j]
        mine = back[h * wide : (h + 1) * wide, :]
        crossed = sum(
            lax.dot_general(lock3[:nlock], x, NT, preferred_element_type=jnp.float32)
            for x in split3(mine)
        )
        return crossed, square

    def scattered(h):
        for name in ("dfar", "dadj", "extra", "dmate", "face", "mate"):
            scatter[h][name].wait_send()
        for flag, names in ((0, ("cadj", "cfar")), (1, ("xadj", "xfar"))):

            @pl.when(mid == flag)
            def _():
                for name in names:
                    scatter[h][name].wait_send()

    collect(1, w0, 0, nblocks)
    scatter_first(0)
    settled(1)
    sweep(u1, rows, tiles, 1, 0, steps // 4)
    beyond_out(0, "far", far, 1)
    beyond_out(0, "adj", adj, 0)
    sweep(u1, rows, tiles, 1, steps // 4, steps // 2)
    near_out(0)
    sweep(u1, rows, tiles, 1, steps // 2, steps * 3 // 4)
    beyond_pass(0, "far", far, 1)
    beyond_pass(0, "adj", adj, 0)
    sweep(u1, rows, tiles, 1, steps * 3 // 4, steps)
    collect(1, w1, 0, nblocks)
    scatter_first(1)
    write_u(0)
    beyond_out(1, "far", far, 1)
    beyond_out(1, "adj", adj, 0)
    near_out(1)
    beyond_pass(1, "far", far, 1)
    beyond_pass(1, "adj", adj, 0)
    crossed0, square0 = total(0)
    write_u(1)
    crossed1, square1 = total(1)
    crossed = jnp.concatenate([crossed0, crossed1], axis=1)
    squares = lax.dot_general(
        jnp.ones((8, TILE), jnp.float32), jnp.concatenate([square0, square1], axis=0), NT,
        precision=HIGH, preferred_element_type=jnp.float32,
    )
    tail = jnp.concatenate(
        [
            jnp.concatenate([crossed[:half], crossed[half:]], axis=1),
            jnp.concatenate([squares, jnp.zeros_like(squares)], axis=1),
        ],
        axis=0,
    )
    pending = start_sum(plane(), tail, last_p, sp2, rp2)
    tail = end_sum(plane(), pending, last_p)
    pending = start_sum(column(), tail, last_c, sc2, rc2)
    for h in range(HALVES):
        all_sent(h)
        exchanged(h)
        scattered(h)
    tail = end_sum(column(), pending, last_c)
    stack = jnp.concatenate([tail[:half, :width], tail[:half, width:], tail[half:, :width]], axis=0)
    stack = jnp.concatenate([stack, jnp.zeros_like(stack)], axis=1).T[:width]
    proj2, backsq = stack[:, :nlock], stack[:, nlock : nlock + 1]
    folded = jnp.dot(proj2, gram, precision=HIGH) - 2.0 * proj2
    colsq = backsq + jnp.sum(proj2 * folded, axis=1, keepdims=True)
    scale = 1.0 / jnp.sqrt(jnp.maximum(colsq, 0.0) / items + 1e-06)
    gone = jnp.dot(
        jnp.concatenate(split3(proj2), axis=1), lock3[...], preferred_element_type=jnp.float32
    )
    v_out[...] = (back[...] - gone) * scale


def one_kernel_plan(v_start, locked, tile_rows, tile_cols, tile_seeds, tile_count):
    n_user, n_item = lax.axis_size("user"), lax.axis_size("item")
    shard, width = v_start.shape
    nlock = locked.shape[1]
    nslots = tile_rows.shape[1]
    nblocks = shard * n_user // TILE
    own = shard // TILE
    wide = width // HALVES
    hop = RB // 2
    bf, fl, i32 = jnp.bfloat16, jnp.float32, jnp.int32
    hbm = pl.BlockSpec(memory_space=pl.ANY)
    slab = pltpu.VMEM((nblocks, wide, TILE), bf)
    users = pltpu.VMEM((RB, wide, TILE), bf)
    trade = pltpu.VMEM((HALVES, hop, wide, TILE), bf)
    rows = nlock // 2 + 8
    u_factor, v_next = pl.pallas_call(
        functools.partial(round_kernel, float(shard * n_user * n_item)),
        name="round",
        out_shape=(
            jax.ShapeDtypeStruct((width, RB // n_item * TILE), bf),
            jax.ShapeDtypeStruct((width, shard), fl),
        ),
        in_specs=[SMEM_SPEC] + [hbm] * 5,
        out_specs=(VMEM_SPEC, VMEM_SPEC),
        scratch_shapes=[
            pltpu.SMEM((1, nslots), i32),
            pltpu.SMEM((1, nslots), i32),
            pltpu.SMEM((1, nslots), i32),
            pltpu.SMEM((8, nslots), i32),
            pltpu.VMEM((1, nslots), i32),
            pltpu.VMEM((1, nslots), i32),
            pltpu.VMEM((8, nslots), i32),
            pltpu.VMEM((width, shard), bf),
            pltpu.VMEM((3 * nlock, shard), bf),
            pltpu.VMEM((nslots, TILE, TILE), bf),
            pltpu.VMEM((nslots, TILE, TILE), bf),
            pltpu.VMEM((nslots + 1, wide, TILE), fl),
            slab, slab, users, users, trade, trade, trade, users, users, slab, slab,
            pltpu.VMEM((HALVES, 8 * own, wide, TILE), bf),
            pltpu.VMEM((HALVES, 4 * own, wide, TILE), bf),
            pltpu.VMEM((width, shard), fl),
            pltpu.VMEM((2 * n_item, rows, TILE), fl),
            pltpu.VMEM((n_user // 2, rows, TILE), fl),
            pltpu.VMEM((2 * n_item, rows, TILE), fl),
            pltpu.VMEM((n_user // 2, rows, TILE), fl),
            sems(8),
            sems(HALVES, 10), sems(HALVES, 10),
            sems(HALVES, 3, PARTS), sems(HALVES, 3, PARTS),
            sems(HALVES, 10), sems(HALVES, 10),
        ]
        + ([sems(2 * n_item - 1)] * 2 + [sems(n_user // 2 - 1)] * 2) * 2,
        compiler_params=pltpu.CompilerParams(
            collective_id=0, has_side_effects=True, vmem_limit_bytes=BIG_LIMIT
        ),
    )(tile_count, tile_rows, tile_cols, tile_seeds, v_start.T, locked.T)
    return u_factor.T, v_next.T


def fits_one_kernel(v_start, locked, tile_rows):
    return (
        v_start.shape[0] % (2 * TILE) == 0
        and v_start.shape[1] == 64
        and locked.shape[1] == 32
        and tile_rows.shape[1] % 512 == 0
        and lax.axis_size("item") == 4
        and lax.axis_size("user") == 8
    )


def on_device(v_start, locked, tile_rows, tile_cols, tile_seeds, tile_count):
    if fits_one_kernel(v_start, locked, tile_rows):
        return one_kernel_plan(v_start, locked, tile_rows, tile_cols, tile_seeds, tile_count)
    both = ("user", "item")
    lockf = locked.astype(jnp.float32)
    nlock = locked.shape[1]
    n_user, n_item = lax.axis_size("user"), lax.axis_size("item")
    slab = v_start.shape[0] * n_user
    stats = jnp.dot(
        locked.T, jnp.concatenate([v_start, locked], axis=1), preferred_element_type=jnp.float32
    )
    stats = lax.psum(stats, both)
    proj, gram = stats[:, :-nlock], stats[:, -nlock:]
    deflated = (v_start.astype(jnp.float32) - jnp.dot(lockf, proj, precision=HIGH)).astype(
        jnp.bfloat16
    )
    vslab = lax.all_gather(deflated, "user", axis=0, tiled=True)
    places = pack(tile_rows, tile_cols)
    flipped, tiles = [
        pl.pallas_call(
            functools.partial(fill_kernel, flip),
            name="fill",
            out_shape=jax.ShapeDtypeStruct((tile_seeds.shape[1], TILE, TILE), jnp.bfloat16),
            in_specs=[SMEM_SPEC],
            out_specs=VMEM_SPEC,
            compiler_params=pltpu.CompilerParams(vmem_limit_bytes=LIMIT),
        )(tile_seeds)
        for flip in (True, False)
    ]
    upart = product(True, places, tile_count, blocks_of(vslab), flipped, RB, jnp.float32)
    ublocks = lax.psum(upart, "item").astype(jnp.bfloat16)
    per = RB // n_item
    u_factor = rows_of(lax.dynamic_slice_in_dim(ublocks, lax.axis_index("item") * per, per, 0))
    wpart = product(False, places, tile_count, ublocks, tiles, slab // TILE, jnp.float32)
    back = lax.psum_scatter(rows_of(wpart), "user", scatter_dimension=0, tiled=True)
    sums = jnp.concatenate(
        [jnp.dot(lockf.T, back, precision=HIGH), jnp.sum(back * back, axis=0)[None]], axis=0
    )
    sums = lax.psum(sums, both)
    proj2, backsq = sums[:-1], sums[-1]
    rest = back - jnp.dot(lockf, proj2, precision=HIGH)
    crossed = jnp.dot(gram, proj2, precision=HIGH) - 2.0 * proj2
    colsq = jnp.maximum(backsq + jnp.sum(proj2 * crossed, axis=0), 0.0)
    v_next = rest / jnp.sqrt(colsq / (slab * n_item) + 1e-06)
    return (u_factor, v_next)


def solution(mesh):
    spec = P(("user", "item"), None)
    return jax.shard_map(
        on_device, mesh=mesh, in_specs=(spec,) * 6, out_specs=(spec, spec), check_vma=False
    )
```

```python
import functools

import jax
import jax.numpy as jnp
from jax import lax
from jax.experimental import pallas as pl
from jax.experimental.pallas import tpu as pltpu
from jax.sharding import PartitionSpec as P

TILE = 128
RB = 64
LIMIT = 16 << 20
BIG_LIMIT = 56 << 20
GROUP = 16
SPAN = 32
SCALE = 1.0 / 1024.0
HIGH = lax.Precision.HIGHEST
NT = (((1,), (1,)), ((), ()))
NN = (((1,), (0,)), ((), ()))


def fill(seeds, tiles_ref, first, last, flip):
    a = lax.broadcasted_iota(jnp.int32, (TILE, TILE), 0)
    b = lax.broadcasted_iota(jnp.int32, (TILE, TILE), 1)
    base = (b * TILE + a if flip else a * TILE + b) * 40503

    def step(g, carry):
        for j in range(GROUP):
            s = g * GROUP + j
            h = base + seeds[0, s] * 9973
            h = h ^ (h >> 13)
            h = h * 1597334677
            h = h ^ (h >> 16)
            levels = ((h >> 8) & 255) - 128
            tiles_ref[s] = levels.astype(jnp.float32).astype(jnp.bfloat16)
        return carry

    lax.fori_loop(first, last, step, 0)


def fill_kernel(flip, seeds, tiles_ref):
    fill(seeds, tiles_ref, 0, tiles_ref.shape[0] // GROUP, flip)


def product_kernel(forward, places, count, x_ref, tiles_ref, out_ref, acc):
    blocks = out_ref.shape[0]
    live = count[0, 0]
    acc[...] = jnp.zeros_like(acc)

    def step(g, carry):
        for j in range(SPAN):
            s = g * SPAN + j
            row, col = places[0, s] >> 16, places[0, s] & 65535
            source, target = (col, row) if forward else (row, col)
            target = jnp.where(s < live, target, blocks)
            acc[target] += lax.dot_general(
                x_ref[source], tiles_ref[s], NN, preferred_element_type=jnp.float32
            )
        return carry

    lax.fori_loop(0, lax.div(live + (SPAN - 1), SPAN), step, 0)
    out_ref[...] = (acc[:blocks] * SCALE).astype(out_ref.dtype)


VMEM_SPEC = pl.BlockSpec(memory_space=pltpu.VMEM)
SMEM_SPEC = pl.BlockSpec(memory_space=pltpu.SMEM)


def product(forward, places, count, x, tiles, nblocks, dtype):
    width, tile = x.shape[1:]
    return pl.pallas_call(
        functools.partial(product_kernel, forward),
        name="forward" if forward else "backward",
        out_shape=jax.ShapeDtypeStruct((nblocks, width, tile), dtype),
        in_specs=[SMEM_SPEC, SMEM_SPEC, VMEM_SPEC, VMEM_SPEC],
        out_specs=VMEM_SPEC,
        scratch_shapes=[pltpu.VMEM((nblocks + 1, width, tile), jnp.float32)],
        compiler_params=pltpu.CompilerParams(vmem_limit_bytes=LIMIT),
    )(places, count, x, tiles)


def blocks_of(x):
    return x.reshape(-1, TILE, x.shape[1]).transpose(0, 2, 1)


def rows_of(blocks):
    return blocks.transpose(0, 2, 1).reshape(-1, blocks.shape[1])


MESH = pl.DeviceIdType.MESH


def place():
    user = lax.axis_index("user")
    return lax.div(user, 2), lax.rem(user, 2), lax.axis_index("item")


def plane():
    z, y, item = place()
    n = 2 * lax.axis_size("item")
    me = y * lax.axis_size("item") + item
    out = []
    for o in range(1, n):
        p = lax.rem(me + o, n)
        out.append({"user": 2 * z + lax.div(p, n // 2), "item": lax.rem(p, n // 2)})
    return n, me, out


def column():
    z, y, item = place()
    n = lax.axis_size("user") // 2
    return n, z, [{"user": 2 * lax.rem(z + o, n) + y, "item": item} for o in range(1, n)]


def remote(src, dst, send, recv, device):
    return pltpu.make_async_remote_copy(
        src_ref=src, dst_ref=dst, send_sem=send, recv_sem=recv, device_id=device,
        device_id_type=MESH,
    )


def sems(*shape):
    return pltpu.SemaphoreType.DMA(shape)


def pack(tile_rows, tile_cols):
    return tile_rows * 65536 + tile_cols


HALVES = 2
PARTS = 4
PIECES = 2
WIDE_GROUP = 128


def split3(x):
    high = x.astype(jnp.bfloat16)
    rest = x - high.astype(jnp.float32)
    mid = rest.astype(jnp.bfloat16)
    low = (rest - mid.astype(jnp.float32)).astype(jnp.bfloat16)
    return high, mid, low


def f32(x):
    return x.astype(jnp.float32)


def start_sum(group, value, slots, send, recv):
    n, me, devices = group
    slots[me] = value
    copies = [
        remote(slots.at[me], slots.at[me], send.at[o], recv.at[o], device)
        for o, device in enumerate(devices)
    ]
    for copy in copies:
        copy.start()
    return copies


def end_sum(group, copies, slots):
    for copy in copies:
        copy.wait()
    total = slots[0]
    for i in range(1, group[0]):
        total = total + slots[i]
    return total


def round_kernel(
    items, count, rows_hbm, cols_hbm, seeds_hbm, v_hbm, lock_hbm, u_out, v_out,
    rows, cols, seeds, links, row_lanes, col_lanes, link_lanes, v_ref, lock3,
    tiles, flipped, sums, v0, v1, part0, part1, near, pair, far_part, u0, u1, w0, w1,
    inbox, outbox, back, slots_p, slots_c, last_p, last_c,
    in_sem, ag_s, ag_r, x_s, x_r, rs_s, rs_r, sp, rp, sc, rc, sp2, rp2, sc2, rc2,
):
    vbuf, part, ubuf, wbuf = (v0, v1), (part0, part1), (u0, u1), (w0, w1)
    nslots = tiles.shape[0]
    nlock = lock_hbm.shape[0]
    width = v_hbm.shape[0]
    wide = width // HALVES
    own = v_hbm.shape[1] // TILE
    cut = own // PIECES
    nblocks = v0.shape[0]
    z, y, item = place()
    side = lax.rem(item, 2)
    upper = lax.div(z, 2)
    mate = z + 1 - 2 * lax.rem(z, 2)
    adj, far = 2 - upper, 3 - 3 * upper
    mid = 1 - lax.div(lax.rem(z + 2, 3), 2)
    user = 2 * z + y

    def at(zz, yy):
        return {"user": 2 * zz + yy, "item": item}

    facing_dev, mate_dev, adj_dev, far_dev = at(z, 1 - y), at(mate, y), at(adj, y), at(far, y)
    sibling = {"user": user, "item": item + 1 - 2 * side}
    across = {"user": user, "item": lax.rem(item + 2, 4)}

    loads = [
        pltpu.make_async_copy(src, dst, in_sem.at[i])
        for i, (src, dst) in enumerate(
            (
                (v_hbm, v_ref),
                (lock_hbm, lock3.at[pl.ds(0, nlock)]),
                (rows_hbm, row_lanes),
                (cols_hbm, col_lanes),
                (rows_hbm, rows),
                (cols_hbm, cols),
                (seeds_hbm, seeds),
            )
        )
    ]
    for load in loads:
        load.start()
    barrier = pltpu.get_barrier_semaphore()
    peers = plane()[2] + column()[2]
    for device in peers:
        pl.semaphore_signal(barrier, inc=1, device_id=device, device_id_type=MESH)
    sums[nslots] = jnp.zeros((wide, TILE), jnp.float32)
    for load in loads:
        load.wait()
    lock = lock3[:nlock]
    lock3[nlock : 2 * nlock] = lock
    lock3[2 * nlock : 3 * nlock] = lock
    proj = lax.dot_general(lock, v_ref[...], NT, preferred_element_type=jnp.float32)
    gram = lax.dot_general(lock, lock, NT, preferred_element_type=jnp.float32)
    half = nlock // 2
    quarter = nlock // 4
    stats = jnp.concatenate(
        [
            jnp.concatenate([proj[:half], proj[half:]], axis=1),
            jnp.concatenate([gram[i * quarter : (i + 1) * quarter] for i in range(4)], axis=1),
        ],
        axis=0,
    )
    pl.semaphore_wait(barrier, len(peers))
    pending = start_sum(plane(), stats, slots_p, sp, rp)

    live = count[0, 0]
    slot_lane = lax.broadcasted_iota(jnp.int32, (TILE, nslots), 1)
    slot_row = lax.broadcasted_iota(jnp.int32, (TILE, nslots), 0)
    block_lane = lax.broadcasted_iota(jnp.int32, (TILE, TILE), 1)
    block_row = lax.broadcasted_iota(jnp.int32, (TILE, TILE), 0)
    for which, lanes in enumerate((row_lanes, col_lanes)):
        wide_lanes = jnp.broadcast_to(lanes[...], (TILE, nslots))
        previous = jnp.full((1, nslots), -1, jnp.int32)
        latest = jnp.full((1, TILE), -1, jnp.int32)
        for j in range(nslots // TILE):
            down = wide_lanes[:, j * TILE : (j + 1) * TILE].T
            here = slot_row + j * TILE
            hit = (jnp.tile(down, (1, nslots // TILE)) == wide_lanes) & (here < slot_lane)
            hit = jnp.where(hit & (here < live), here, -1)
            previous = jnp.maximum(previous, jnp.max(hit, axis=0, keepdims=True))
            here = block_row + j * TILE
            hit = jnp.where((down == block_lane) & (here < live), here, -1)
            latest = jnp.maximum(latest, jnp.max(hit, axis=0, keepdims=True))
        link_lanes[which : which + 1, :] = jnp.where(previous < 0, nslots, previous)
        link_lanes[2 + which : 3 + which, :TILE] = jnp.where(latest < 0, nslots, latest)
    place_links = pltpu.make_async_copy(link_lanes, links, in_sem.at[len(loads)])
    place_links.start()

    iota_a = lax.broadcasted_iota(jnp.int32, (TILE, TILE), 0)
    iota_b = lax.broadcasted_iota(jnp.int32, (TILE, TILE), 1)
    base = (iota_a * TILE + iota_b) * 40503

    def fill_some(first, last):
        def step(g, carry):
            for j in range(GROUP):
                s = g * GROUP + j
                h = base + seeds[0, s] * 9973
                h = h ^ (h >> 13)
                h = h * 1597334677
                h = h ^ (h >> 16)
                levels = (((h >> 8) & 255) - 128).astype(jnp.float32).astype(jnp.bfloat16)
                tiles[s] = levels
                flipped[s] = levels.T
            return carry

        lax.fori_loop(first, last, step, 0)

    groups = nslots // GROUP
    marks = [groups * i // 32 for i in (0, 6, 13, 17, 19, 21, 23, 26, 28, 32)]
    fill_some(marks[0], marks[1])
    stats = end_sum(plane(), pending, slots_p)
    pending = start_sum(column(), stats, slots_c, sc, rc)
    fill_some(marks[1], marks[2])
    stats = end_sum(column(), pending, slots_c)
    gram = jnp.concatenate(
        [stats[half : half + quarter, i * nlock : (i + 1) * nlock] for i in range(4)], axis=0
    )
    proj = jnp.concatenate([stats[:half, :width], stats[:half, width:]], axis=0)
    projt = jnp.concatenate([proj, jnp.zeros_like(proj)], axis=1).T[:width]
    gone = jnp.dot(
        jnp.concatenate(split3(projt), axis=1), lock3[...], preferred_element_type=jnp.float32
    )
    deflated = (f32(v_ref[...]) - gone).astype(jnp.bfloat16)
    for h in range(HALVES):
        for j in range(own):
            vbuf[h][user * own + j] = deflated[h * wide : (h + 1) * wide, j * TILE : (j + 1) * TILE]

    def spread(h, zz, yy, si, ri, device, k):
        ref = vbuf[h].at[pl.ds((2 * zz + yy) * own + k * cut, cut)]
        return remote(ref, ref, ag_s.at[h, si, k], ag_r.at[h, ri, k], device)

    routes = dict(
        face=(z, y, 0, 0, facing_dev),
        cross=(z, y, 1, 2 - mid, adj_dev),
        mate=(z, y, 3, 3, mate_dev),
        dmate=(mate, y, 4, 4, facing_dev),
        dadj=(adj, y, 5, 5, facing_dev),
        dfar=(far, y, 6, 6, facing_dev),
        extra=(z, 1 - y, 7, 7, mate_dev),
        cadj=(adj, y, 8, 1, mate_dev),
        cfar=(far, y, 9, 2, mate_dev),
    )

    def gather(h, name, k):
        return spread(h, *routes[name], k)

    def own_out(h):
        for k in range(PIECES):
            for name in ("cross", "face", "mate"):
                gather(h, name, k).start()

    def near_in(h):
        gather(h, "mate", 0).wait_recv()
        gather(h, "dmate", 0).start()
        gather(h, "face", 1).wait_recv()
        gather(h, "extra", 1).start()

    def beyond_in(h, k):
        for name in ("adj", "far"):
            gather(h, "c" + name, k).wait_recv()

            @pl.when(mid == 1)
            def _():
                gather(h, "c" + name, k).start()

            gather(h, "d" + name, k).start()

    def rest_in(h):
        gather(h, "mate", 1).wait_recv()
        gather(h, "face", 0).wait_recv()
        gather(h, "extra", 1).wait_recv()
        gather(h, "dmate", 0).wait_recv()
        for k in range(PIECES):
            for name in ("dadj", "dfar"):
                gather(h, name, k).wait_recv()

    def all_sent(h):
        gather(h, "extra", 1).wait_send()
        gather(h, "dmate", 0).wait_send()
        for k in range(PIECES):
            for name in ("face", "cross", "mate", "dadj", "dfar"):
                gather(h, name, k).wait_send()

        @pl.when(mid == 1)
        def _():
            for k in range(PIECES):
                gather(h, "cadj", k).wait_send()
                gather(h, "cfar", k).wait_send()

    own_out(0)
    own_out(1)
    fill_some(marks[2], marks[3])
    near_in(0)
    fill_some(marks[3], marks[4])
    beyond_in(0, 0)
    fill_some(marks[4], marks[5])
    beyond_in(0, 1)
    fill_some(marks[5], marks[6])
    near_in(1)
    fill_some(marks[6], marks[7])
    beyond_in(1, 0)
    fill_some(marks[7], marks[8])
    beyond_in(1, 1)
    fill_some(marks[8], marks[9])
    place_links.wait()
    rest_in(0)

    def sweep(x, blocks, weights, which, first, last):
        zero = jnp.zeros((wide, TILE), jnp.bfloat16)

        def step(g, carry):
            for j in range(WIDE_GROUP // 2):
                s = g * WIDE_GROUP + 2 * j
                x0 = jnp.concatenate([x[blocks[0, s]], zero], axis=1)
                x1 = jnp.concatenate([zero, x[blocks[0, s + 1]]], axis=1)
                both = lax.dot_general(
                    jnp.concatenate([x0, x1], axis=0),
                    weights[pl.ds(s, 2)].reshape(2 * TILE, TILE),
                    NN,
                    preferred_element_type=jnp.float32,
                )
                sums[s] = sums[links[which, s]] + both[:wide]
                sums[s + 1] = sums[links[which, s + 1]] + both[wide:]
            return carry

        lax.fori_loop(first, last, step, 0)

    def collect(which, out, first, size):
        def step(g, carry):
            for j in range(8):
                r = first + g * 8 + j
                out[r] = (sums[links[2 + which, r]] * SCALE).astype(out.dtype)
            return carry

        lax.fori_loop(0, size // 8, step, 0)

    steps = nslots // WIDE_GROUP
    hop = RB // 2
    size = hop // PARTS

    def exchange(h, k):
        def one(i, src, src_at, dst, dst_at, device):
            return remote(
                src.at[pl.ds(src_at + k * size, size)],
                dst.at[pl.ds(dst_at + k * size, size)],
                x_s.at[h, i, k],
                x_r.at[h, i, k],
                device,
            )

        return (
            one(0, part[h], (1 - side) * hop, near.at[h], 0, sibling),
            one(1, pair.at[h], 0, far_part.at[h], 0, across),
            one(2, ubuf[h], side * hop, ubuf[h], side * hop, sibling),
        )

    def give(h):
        collect(0, part[h], (1 - side) * hop, hop)
        for k in range(PARTS):
            exchange(h, k)[0].start()
        collect(0, part[h], side * hop, hop)

    def swap(h, k):
        given, swapped, _ = exchange(h, k)
        given.wait_recv()
        mine = part[h][pl.ds(side * hop + k * size, size)]
        span = pl.ds(k * size, size)
        pair[h, span] = (f32(mine) + f32(near[h, span])).astype(pair.dtype)
        swapped.start()

    def settle(h, k):
        _, swapped, backward = exchange(h, k)
        swapped.wait_recv()
        span = pl.ds(k * size, size)
        total = f32(pair[h, span]) + f32(far_part[h, span])
        ubuf[h][pl.ds(side * hop + k * size, size)] = total.astype(jnp.bfloat16)
        backward.start()

    def settled(h):
        for k in range(PARTS):
            exchange(h, k)[2].wait_recv()

    def exchanged(h):
        for k in range(PARTS):
            for copy in exchange(h, k):
                copy.wait_send()

    per = RB // 4

    def write_u(h):
        for j in range(per):
            u_out[h * wide : (h + 1) * wide, j * TILE : (j + 1) * TILE] = ubuf[h][item * per + j]

    sweep(v0, cols, flipped, 0, 0, steps)
    give(0)

    def first_swaps(k, carry):
        swap(0, k)
        return carry

    lax.fori_loop(0, PARTS, first_swaps, 0)
    rest_in(1)
    sweep(v1, cols, flipped, 0, 0, steps)
    give(1)

    def second_swaps(k, carry):
        swap(1, k)
        settle(0, k)
        return carry

    lax.fori_loop(0, PARTS, second_swaps, 0)
    settled(0)
    sweep(u0, rows, tiles, 1, 0, steps)

    def piece(h, zz, yy, k):
        return wbuf[h].at[pl.ds((2 * zz + yy) * own + k * cut, cut)]

    def stage(h, i, k):
        return outbox.at[h, pl.ds(i * own + k * cut, cut)]

    box = dict(dmate=0, extra=0, dadj=1, dfar=2, cadj=3, cfar=4, mate=5, cross=6, face=7)
    posts = dict(
        dfar=((far, 1 - y), None, 0, 0, facing_dev),
        dadj=((adj, 1 - y), None, 1, 1, facing_dev),
        extra=((mate, 1 - y), None, 2, 2, mate_dev),
        dmate=((mate, 1 - y), None, 3, 3, facing_dev),
        cadj=(None, 0, 4, 4, mate_dev),
        cfar=(None, 1, 5, 5, mate_dev),
        xadj=(None, 0, 6, 6, adj_dev),
        xfar=(None, 1, 7, 6, far_dev),
        face=((z, 1 - y), 2, 8, 8, facing_dev),
        mate=((mate, y), 3, 9, 9, mate_dev),
    )
    direct = (("face", 0), ("mate", 1))

    def scatter(h, name, k):
        where, slot, si, ri, device = posts[name]
        staged = slot is not None and (name, k) not in direct
        src = stage(h, slot, k) if staged else piece(h, *where, k)
        first = box["cross" if name[0] == "x" else name] * own + k * cut
        return remote(
            src, inbox.at[h, pl.ds(first, cut)], rs_s.at[h, si, k], rs_r.at[h, ri, k], device
        )

    def scatter_first(h):
        for k in range(PIECES):
            scatter(h, "dfar", k).start()
            scatter(h, "dadj", k).start()
        scatter(h, "extra", 1).start()
        scatter(h, "dmate", 0).start()
        scatter(h, "mate", 1).start()
        scatter(h, "face", 0).start()

    def got(h, name, k):
        return f32(inbox[h, box[name] * own + k * cut : box[name] * own + (k + 1) * cut])

    def block(h, zz, yy, k):
        return f32(wbuf[h][pl.ds((2 * zz + yy) * own + k * cut, cut)])

    def put(h, i, k, value):
        outbox[h, i * own + k * cut : i * own + (k + 1) * cut] = value.astype(outbox.dtype)

    def beyond_out(h, k):
        for name, zz, i in (("far", far, 1), ("adj", adj, 0)):
            scatter(h, "d" + name, k).wait_recv()

            @pl.when(mid == 0)
            def _():
                put(h, i, k, block(h, zz, y, k) + got(h, "d" + name, k))
                scatter(h, "c" + name, k).start()

    def beyond_pass(h, k):
        @pl.when(mid == 1)
        def _():
            for name, zz, i in (("far", far, 1), ("adj", adj, 0)):
                scatter(h, "c" + name, k).wait_recv()
                both = block(h, zz, y, k) + got(h, "d" + name, k) + got(h, "c" + name, k)
                put(h, i, k, both)
                scatter(h, "x" + name, k).start()

    def near_out(h):
        scatter(h, "extra", 1).wait_recv()
        put(h, 2, 1, block(h, z, 1 - y, 1) + got(h, "extra", 1))
        scatter(h, "face", 1).start()
        scatter(h, "dmate", 0).wait_recv()
        put(h, 3, 0, block(h, mate, y, 0) + got(h, "dmate", 0))
        scatter(h, "mate", 0).start()

    def total(h):
        square = jnp.zeros((wide, TILE), jnp.float32)
        for k in range(PIECES):
            scatter(h, "mate", k).wait_recv()
            scatter(h, "face", k).wait_recv()
            scatter(h, "xadj", k).wait_recv()
            whole = block(h, z, y, k) + got(h, "mate", k) + got(h, "face", k) + got(h, "cross", k)
            for j in range(cut):
                lane = (k * cut + j) * TILE
                back[h * wide : (h + 1) * wide, lane : lane + TILE] = whole[j]
                square = square + whole[j] * whole[j]
        mine = back[h * wide : (h + 1) * wide, :]
        crossed = sum(
            lax.dot_general(lock3[:nlock], x, NT, preferred_element_type=jnp.float32)
            for x in split3(mine)
        )
        return crossed, square

    def scattered(h):
        scatter(h, "extra", 1).wait_send()
        scatter(h, "dmate", 0).wait_send()
        for k in range(PIECES):
            for name in ("dfar", "dadj", "face", "mate"):
                scatter(h, name, k).wait_send()
        for flag, names in ((0, ("cadj", "cfar")), (1, ("xadj", "xfar"))):

            @pl.when(mid == flag)
            def _():
                for k in range(PIECES):
                    for name in names:
                        scatter(h, name, k).wait_send()

    collect(1, w0, 0, nblocks)
    scatter_first(0)
    for k in range(PARTS):
        settle(1, k)
    beyond_out(0, 0)
    beyond_out(0, 1)
    settled(1)
    sweep(u1, rows, tiles, 1, 0, steps // 4)
    near_out(0)
    sweep(u1, rows, tiles, 1, steps // 4, steps // 2)
    beyond_pass(0, 0)
    sweep(u1, rows, tiles, 1, steps // 2, steps * 3 // 4)
    beyond_pass(0, 1)
    sweep(u1, rows, tiles, 1, steps * 3 // 4, steps)
    collect(1, w1, 0, nblocks)
    scatter_first(1)
    write_u(0)
    beyond_out(1, 0)
    beyond_out(1, 1)
    beyond_pass(1, 0)
    near_out(1)
    beyond_pass(1, 1)
    crossed0, square0 = total(0)
    write_u(1)
    crossed1, square1 = total(1)
    crossed = jnp.concatenate([crossed0, crossed1], axis=1)
    squares = lax.dot_general(
        jnp.ones((8, TILE), jnp.float32), jnp.concatenate([square0, square1], axis=0), NT,
        precision=HIGH, preferred_element_type=jnp.float32,
    )
    tail = jnp.concatenate(
        [
            jnp.concatenate([crossed[:half], crossed[half:]], axis=1),
            jnp.concatenate([squares, jnp.zeros_like(squares)], axis=1),
        ],
        axis=0,
    )
    pending = start_sum(plane(), tail, last_p, sp2, rp2)
    tail = end_sum(plane(), pending, last_p)
    pending = start_sum(column(), tail, last_c, sc2, rc2)
    for h in range(HALVES):
        all_sent(h)
        exchanged(h)
        scattered(h)
    tail = end_sum(column(), pending, last_c)
    stack = jnp.concatenate([tail[:half, :width], tail[:half, width:], tail[half:, :width]], axis=0)
    stack = jnp.concatenate([stack, jnp.zeros_like(stack)], axis=1).T[:width]
    proj2, backsq = stack[:, :nlock], stack[:, nlock : nlock + 1]
    folded = jnp.dot(proj2, gram, precision=HIGH) - 2.0 * proj2
    colsq = backsq + jnp.sum(proj2 * folded, axis=1, keepdims=True)
    scale = 1.0 / jnp.sqrt(jnp.maximum(colsq, 0.0) / items + 1e-06)
    gone = jnp.dot(
        jnp.concatenate(split3(proj2), axis=1), lock3[...], preferred_element_type=jnp.float32
    )
    v_out[...] = (back[...] - gone) * scale


def one_kernel_plan(v_start, locked, tile_rows, tile_cols, tile_seeds, tile_count):
    n_user, n_item = lax.axis_size("user"), lax.axis_size("item")
    shard, width = v_start.shape
    nlock = locked.shape[1]
    nslots = tile_rows.shape[1]
    nblocks = shard * n_user // TILE
    own = shard // TILE
    wide = width // HALVES
    hop = RB // 2
    bf, fl, i32 = jnp.bfloat16, jnp.float32, jnp.int32
    hbm = pl.BlockSpec(memory_space=pl.ANY)
    slab = pltpu.VMEM((nblocks, wide, TILE), bf)
    users = pltpu.VMEM((RB, wide, TILE), bf)
    trade = pltpu.VMEM((HALVES, hop, wide, TILE), bf)
    rows = nlock // 2 + 8
    u_factor, v_next = pl.pallas_call(
        functools.partial(round_kernel, float(shard * n_user * n_item)),
        name="round",
        out_shape=(
            jax.ShapeDtypeStruct((width, RB // n_item * TILE), bf),
            jax.ShapeDtypeStruct((width, shard), fl),
        ),
        in_specs=[SMEM_SPEC] + [hbm] * 5,
        out_specs=(VMEM_SPEC, VMEM_SPEC),
        scratch_shapes=[
            pltpu.SMEM((1, nslots), i32),
            pltpu.SMEM((1, nslots), i32),
            pltpu.SMEM((1, nslots), i32),
            pltpu.SMEM((8, nslots), i32),
            pltpu.VMEM((1, nslots), i32),
            pltpu.VMEM((1, nslots), i32),
            pltpu.VMEM((8, nslots), i32),
            pltpu.VMEM((width, shard), bf),
            pltpu.VMEM((3 * nlock, shard), bf),
            pltpu.VMEM((nslots, TILE, TILE), bf),
            pltpu.VMEM((nslots, TILE, TILE), bf),
            pltpu.VMEM((nslots + 1, wide, TILE), fl),
            slab, slab, users, users, trade, trade, trade, users, users, slab, slab,
            pltpu.VMEM((HALVES, 8 * own, wide, TILE), bf),
            pltpu.VMEM((HALVES, 4 * own, wide, TILE), bf),
            pltpu.VMEM((width, shard), fl),
            pltpu.VMEM((2 * n_item, rows, TILE), fl),
            pltpu.VMEM((n_user // 2, rows, TILE), fl),
            pltpu.VMEM((2 * n_item, rows, TILE), fl),
            pltpu.VMEM((n_user // 2, rows, TILE), fl),
            sems(8),
            sems(HALVES, 10, PIECES), sems(HALVES, 10, PIECES),
            sems(HALVES, 3, PARTS), sems(HALVES, 3, PARTS),
            sems(HALVES, 10, PIECES), sems(HALVES, 10, PIECES),
        ]
        + ([sems(2 * n_item - 1)] * 2 + [sems(n_user // 2 - 1)] * 2) * 2,
        compiler_params=pltpu.CompilerParams(
            collective_id=0, has_side_effects=True, vmem_limit_bytes=BIG_LIMIT
        ),
    )(tile_count, tile_rows, tile_cols, tile_seeds, v_start.T, locked.T)
    return u_factor.T, v_next.T


def fits_one_kernel(v_start, locked, tile_rows):
    return (
        v_start.shape[0] % (2 * TILE) == 0
        and v_start.shape[1] == 64
        and locked.shape[1] == 32
        and tile_rows.shape[1] % 512 == 0
        and lax.axis_size("item") == 4
        and lax.axis_size("user") == 8
    )


def on_device(v_start, locked, tile_rows, tile_cols, tile_seeds, tile_count):
    if fits_one_kernel(v_start, locked, tile_rows):
        return one_kernel_plan(v_start, locked, tile_rows, tile_cols, tile_seeds, tile_count)
    both = ("user", "item")
    lockf = locked.astype(jnp.float32)
    nlock = locked.shape[1]
    n_user, n_item = lax.axis_size("user"), lax.axis_size("item")
    slab = v_start.shape[0] * n_user
    stats = jnp.dot(
        locked.T, jnp.concatenate([v_start, locked], axis=1), preferred_element_type=jnp.float32
    )
    stats = lax.psum(stats, both)
    proj, gram = stats[:, :-nlock], stats[:, -nlock:]
    deflated = (v_start.astype(jnp.float32) - jnp.dot(lockf, proj, precision=HIGH)).astype(
        jnp.bfloat16
    )
    vslab = lax.all_gather(deflated, "user", axis=0, tiled=True)
    places = pack(tile_rows, tile_cols)
    flipped, tiles = [
        pl.pallas_call(
            functools.partial(fill_kernel, flip),
            name="fill",
            out_shape=jax.ShapeDtypeStruct((tile_seeds.shape[1], TILE, TILE), jnp.bfloat16),
            in_specs=[SMEM_SPEC],
            out_specs=VMEM_SPEC,
            compiler_params=pltpu.CompilerParams(vmem_limit_bytes=LIMIT),
        )(tile_seeds)
        for flip in (True, False)
    ]
    upart = product(True, places, tile_count, blocks_of(vslab), flipped, RB, jnp.float32)
    ublocks = lax.psum(upart, "item").astype(jnp.bfloat16)
    per = RB // n_item
    u_factor = rows_of(lax.dynamic_slice_in_dim(ublocks, lax.axis_index("item") * per, per, 0))
    wpart = product(False, places, tile_count, ublocks, tiles, slab // TILE, jnp.float32)
    back = lax.psum_scatter(rows_of(wpart), "user", scatter_dimension=0, tiled=True)
    sums = jnp.concatenate(
        [jnp.dot(lockf.T, back, precision=HIGH), jnp.sum(back * back, axis=0)[None]], axis=0
    )
    sums = lax.psum(sums, both)
    proj2, backsq = sums[:-1], sums[-1]
    rest = back - jnp.dot(lockf, proj2, precision=HIGH)
    crossed = jnp.dot(gram, proj2, precision=HIGH) - 2.0 * proj2
    colsq = jnp.maximum(backsq + jnp.sum(proj2 * crossed, axis=0), 0.0)
    v_next = rest / jnp.sqrt(colsq / (slab * n_item) + 1e-06)
    return (u_factor, v_next)


def solution(mesh):
    spec = P(("user", "item"), None)
    return jax.shard_map(
        on_device, mesh=mesh, in_specs=(spec,) * 6, out_specs=(spec, spec), check_vma=False
    )
```

```python
import functools

import jax
import jax.numpy as jnp
from jax import lax
from jax.experimental import pallas as pl
from jax.experimental.pallas import tpu as pltpu
from jax.sharding import PartitionSpec as P

TILE = 128
RB = 64
LIMIT = 16 << 20
BIG_LIMIT = 56 << 20
GROUP = 32
SPAN = 32
SCALE = 1.0 / 1024.0
HIGH = lax.Precision.HIGHEST
NT = (((1,), (1,)), ((), ()))
NN = (((1,), (0,)), ((), ()))


def fill(seeds, tiles_ref, first, last, flip):
    a = lax.broadcasted_iota(jnp.int32, (TILE, TILE), 0)
    b = lax.broadcasted_iota(jnp.int32, (TILE, TILE), 1)
    base = (b * TILE + a if flip else a * TILE + b) * 40503

    def step(g, carry):
        for j in range(GROUP):
            s = g * GROUP + j
            h = base + seeds[0, s] * 9973
            h = h ^ (h >> 13)
            h = h * 1597334677
            h = h ^ (h >> 16)
            levels = ((h >> 8) & 255) - 128
            tiles_ref[s] = levels.astype(jnp.float32).astype(jnp.bfloat16)
        return carry

    lax.fori_loop(first, last, step, 0)


def fill_kernel(flip, seeds, tiles_ref):
    fill(seeds, tiles_ref, 0, tiles_ref.shape[0] // GROUP, flip)


def product_kernel(forward, places, count, x_ref, tiles_ref, out_ref, acc):
    blocks = out_ref.shape[0]
    live = count[0, 0]
    acc[...] = jnp.zeros_like(acc)

    def step(g, carry):
        for j in range(SPAN):
            s = g * SPAN + j
            row, col = places[0, s] >> 16, places[0, s] & 65535
            source, target = (col, row) if forward else (row, col)
            target = jnp.where(s < live, target, blocks)
            acc[target] += lax.dot_general(
                x_ref[source], tiles_ref[s], NN, preferred_element_type=jnp.float32
            )
        return carry

    lax.fori_loop(0, lax.div(live + (SPAN - 1), SPAN), step, 0)
    out_ref[...] = (acc[:blocks] * SCALE).astype(out_ref.dtype)


VMEM_SPEC = pl.BlockSpec(memory_space=pltpu.VMEM)
SMEM_SPEC = pl.BlockSpec(memory_space=pltpu.SMEM)


def product(forward, places, count, x, tiles, nblocks, dtype):
    width, tile = x.shape[1:]
    return pl.pallas_call(
        functools.partial(product_kernel, forward),
        name="forward" if forward else "backward",
        out_shape=jax.ShapeDtypeStruct((nblocks, width, tile), dtype),
        in_specs=[SMEM_SPEC, SMEM_SPEC, VMEM_SPEC, VMEM_SPEC],
        out_specs=VMEM_SPEC,
        scratch_shapes=[pltpu.VMEM((nblocks + 1, width, tile), jnp.float32)],
        compiler_params=pltpu.CompilerParams(vmem_limit_bytes=LIMIT),
    )(places, count, x, tiles)


def blocks_of(x):
    return x.reshape(-1, TILE, x.shape[1]).transpose(0, 2, 1)


def rows_of(blocks):
    return blocks.transpose(0, 2, 1).reshape(-1, blocks.shape[1])


MESH = pl.DeviceIdType.MESH


def place():
    user = lax.axis_index("user")
    return lax.div(user, 2), lax.rem(user, 2), lax.axis_index("item")


def plane():
    z, y, item = place()
    n = 2 * lax.axis_size("item")
    me = y * lax.axis_size("item") + item
    out = []
    for o in range(1, n):
        p = lax.rem(me + o, n)
        out.append({"user": 2 * z + lax.div(p, n // 2), "item": lax.rem(p, n // 2)})
    return n, me, out


def column():
    z, y, item = place()
    n = lax.axis_size("user") // 2
    return n, z, [{"user": 2 * lax.rem(z + o, n) + y, "item": item} for o in range(1, n)]


def remote(src, dst, send, recv, device):
    return pltpu.make_async_remote_copy(
        src_ref=src, dst_ref=dst, send_sem=send, recv_sem=recv, device_id=device,
        device_id_type=MESH,
    )


def sems(*shape):
    return pltpu.SemaphoreType.DMA(shape)


def pack(tile_rows, tile_cols):
    return tile_rows * 65536 + tile_cols


HALVES = 2
PARTS = 4
PIECES = 2
WIDE_GROUP = 128


def split3(x):
    high = x.astype(jnp.bfloat16)
    rest = x - high.astype(jnp.float32)
    mid = rest.astype(jnp.bfloat16)
    low = (rest - mid.astype(jnp.float32)).astype(jnp.bfloat16)
    return high, mid, low


def f32(x):
    return x.astype(jnp.float32)


def start_sum(group, value, slots, send, recv):
    n, me, devices = group
    slots[me] = value
    copies = [
        remote(slots.at[me], slots.at[me], send.at[o], recv.at[o], device)
        for o, device in enumerate(devices)
    ]
    for copy in copies:
        copy.start()
    return copies


def end_sum(group, copies, slots):
    for copy in copies:
        copy.wait()
    total = slots[0]
    for i in range(1, group[0]):
        total = total + slots[i]
    return total


def round_kernel(
    items, count, rows_hbm, cols_hbm, seeds_hbm, v_hbm, lock_hbm, u_out, v_out,
    rows, cols, seeds, links, row_lanes, col_lanes, link_lanes, v_ref, lock3,
    tiles, flipped, sums, v0, v1, part0, part1, near, pair, far_part, u0, u1, w0, w1,
    inbox, outbox, back, slots_p, slots_c, last_p, last_c,
    in_sem, ag_s, ag_r, x_s, x_r, rs_s, rs_r, sp, rp, sc, rc, sp2, rp2, sc2, rc2,
):
    vbuf, part, ubuf, wbuf = (v0, v1), (part0, part1), (u0, u1), (w0, w1)
    nslots = tiles.shape[0]
    nlock = lock_hbm.shape[0]
    width = v_hbm.shape[0]
    wide = width // HALVES
    own = v_hbm.shape[1] // TILE
    cut = own // PIECES
    nblocks = v0.shape[0]
    z, y, item = place()
    side = lax.rem(item, 2)
    upper = lax.div(z, 2)
    mate = z + 1 - 2 * lax.rem(z, 2)
    adj, far = 2 - upper, 3 - 3 * upper
    mid = 1 - lax.div(lax.rem(z + 2, 3), 2)
    user = 2 * z + y

    def at(zz, yy):
        return {"user": 2 * zz + yy, "item": item}

    facing_dev, mate_dev, adj_dev, far_dev = at(z, 1 - y), at(mate, y), at(adj, y), at(far, y)
    sibling = {"user": user, "item": item + 1 - 2 * side}
    across = {"user": user, "item": lax.rem(item + 2, 4)}

    loads = [
        pltpu.make_async_copy(src, dst, in_sem.at[i])
        for i, (src, dst) in enumerate(
            (
                (v_hbm, v_ref),
                (lock_hbm, lock3.at[pl.ds(0, nlock)]),
                (rows_hbm, row_lanes),
                (cols_hbm, col_lanes),
                (rows_hbm, rows),
                (cols_hbm, cols),
                (seeds_hbm, seeds),
            )
        )
    ]
    for load in loads:
        load.start()
    barrier = pltpu.get_barrier_semaphore()
    peers = plane()[2] + column()[2]
    for device in peers:
        pl.semaphore_signal(barrier, inc=1, device_id=device, device_id_type=MESH)
    sums[nslots] = jnp.zeros((wide, TILE), jnp.float32)
    for load in loads[:2]:
        load.wait()
    lock = lock3[:nlock]
    lock3[nlock : 2 * nlock] = lock
    lock3[2 * nlock : 3 * nlock] = lock
    proj = lax.dot_general(lock, v_ref[...], NT, preferred_element_type=jnp.float32)
    gram = lax.dot_general(lock, lock, NT, preferred_element_type=jnp.float32)
    half = nlock // 2
    quarter = nlock // 4
    stats = jnp.concatenate(
        [
            jnp.concatenate([proj[:half], proj[half:]], axis=1),
            jnp.concatenate([gram[i * quarter : (i + 1) * quarter] for i in range(4)], axis=1),
        ],
        axis=0,
    )
    pl.semaphore_wait(barrier, len(peers))
    pending = start_sum(plane(), stats, slots_p, sp, rp)
    for load in loads[2:]:
        load.wait()

    iota_a = lax.broadcasted_iota(jnp.int32, (TILE, TILE), 0)
    iota_b = lax.broadcasted_iota(jnp.int32, (TILE, TILE), 1)
    base = (iota_a * TILE + iota_b) * 40503

    def fill_some(first, last):
        def step(g, carry):
            for j in range(GROUP):
                s = g * GROUP + j
                h = base + seeds[0, s] * 9973
                h = h ^ (h >> 13)
                h = h * 1597334677
                h = h ^ (h >> 16)
                levels = (((h >> 8) & 255) - 128).astype(jnp.float32).astype(jnp.bfloat16)
                tiles[s] = levels
                flipped[s] = levels.T
            return carry

        lax.fori_loop(first, last, step, 0)

    groups = nslots // GROUP
    marks = [groups * i // 32 for i in (0, 6, 13, 17, 19, 21, 23, 26, 28, 32)]
    fill_some(marks[0], marks[1])
    stats = end_sum(plane(), pending, slots_p)
    pending = start_sum(column(), stats, slots_c, sc, rc)
    fill_some(marks[1], marks[2])
    stats = end_sum(column(), pending, slots_c)
    gram = jnp.concatenate(
        [stats[half : half + quarter, i * nlock : (i + 1) * nlock] for i in range(4)], axis=0
    )
    proj = jnp.concatenate([stats[:half, :width], stats[:half, width:]], axis=0)
    projt = jnp.concatenate([proj, jnp.zeros_like(proj)], axis=1).T[:width]
    gone = jnp.dot(
        jnp.concatenate(split3(projt), axis=1), lock3[...], preferred_element_type=jnp.float32
    )
    deflated = (f32(v_ref[...]) - gone).astype(jnp.bfloat16)
    for h in range(HALVES):
        for j in range(own):
            vbuf[h][user * own + j] = deflated[h * wide : (h + 1) * wide, j * TILE : (j + 1) * TILE]

    def spread(h, zz, yy, si, ri, device, k):
        ref = vbuf[h].at[pl.ds((2 * zz + yy) * own + k * cut, cut)]
        return remote(ref, ref, ag_s.at[h, si, k], ag_r.at[h, ri, k], device)

    routes = dict(
        face=(z, y, 0, 0, facing_dev),
        cross=(z, y, 1, 2 - mid, adj_dev),
        mate=(z, y, 3, 3, mate_dev),
        dmate=(mate, y, 4, 4, facing_dev),
        dadj=(adj, y, 5, 5, facing_dev),
        dfar=(far, y, 6, 6, facing_dev),
        extra=(z, 1 - y, 7, 7, mate_dev),
        cadj=(adj, y, 8, 1, mate_dev),
        cfar=(far, y, 9, 2, mate_dev),
    )

    def gather(h, name, k):
        return spread(h, *routes[name], k)

    def own_out(h):
        for k in range(PIECES):
            for name in ("cross", "face", "mate"):
                gather(h, name, k).start()

    def near_in(h):
        gather(h, "mate", 0).wait_recv()
        gather(h, "dmate", 0).start()
        gather(h, "face", 1).wait_recv()
        gather(h, "extra", 1).start()

    def beyond_in(h, k):
        for name in ("adj", "far"):
            gather(h, "c" + name, k).wait_recv()

            @pl.when(mid == 1)
            def _():
                gather(h, "c" + name, k).start()

            gather(h, "d" + name, k).start()

    def rest_in(h):
        gather(h, "mate", 1).wait_recv()
        gather(h, "face", 0).wait_recv()
        gather(h, "extra", 1).wait_recv()
        gather(h, "dmate", 0).wait_recv()
        for k in range(PIECES):
            for name in ("dadj", "dfar"):
                gather(h, name, k).wait_recv()

    def all_sent(h):
        gather(h, "extra", 1).wait_send()
        gather(h, "dmate", 0).wait_send()
        for k in range(PIECES):
            for name in ("face", "cross", "mate", "dadj", "dfar"):
                gather(h, name, k).wait_send()

        @pl.when(mid == 1)
        def _():
            for k in range(PIECES):
                gather(h, "cadj", k).wait_send()
                gather(h, "cfar", k).wait_send()

    own_out(0)
    own_out(1)
    live = count[0, 0]
    slot_lane = lax.broadcasted_iota(jnp.int32, (TILE, nslots), 1)
    slot_row = lax.broadcasted_iota(jnp.int32, (TILE, nslots), 0)
    block_lane = lax.broadcasted_iota(jnp.int32, (TILE, TILE), 1)
    block_row = lax.broadcasted_iota(jnp.int32, (TILE, TILE), 0)
    for which, lanes in enumerate((row_lanes, col_lanes)):
        wide_lanes = jnp.broadcast_to(lanes[...], (TILE, nslots))
        previous = jnp.full((1, nslots), -1, jnp.int32)
        latest = jnp.full((1, TILE), -1, jnp.int32)
        for j in range(nslots // TILE):
            down = wide_lanes[:, j * TILE : (j + 1) * TILE].T
            here = slot_row + j * TILE
            hit = (jnp.tile(down, (1, nslots // TILE)) == wide_lanes) & (here < slot_lane)
            hit = jnp.where(hit & (here < live), here, -1)
            previous = jnp.maximum(previous, jnp.max(hit, axis=0, keepdims=True))
            here = block_row + j * TILE
            hit = jnp.where((down == block_lane) & (here < live), here, -1)
            latest = jnp.maximum(latest, jnp.max(hit, axis=0, keepdims=True))
        link_lanes[which : which + 1, :] = jnp.where(previous < 0, nslots, previous)
        link_lanes[2 + which : 3 + which, :TILE] = jnp.where(latest < 0, nslots, latest)
    place_links = pltpu.make_async_copy(link_lanes, links, in_sem.at[len(loads)])
    place_links.start()
    fill_some(marks[2], marks[3])
    near_in(0)
    fill_some(marks[3], marks[4])
    beyond_in(0, 0)
    fill_some(marks[4], marks[5])
    beyond_in(0, 1)
    fill_some(marks[5], marks[6])
    near_in(1)
    fill_some(marks[6], marks[7])
    beyond_in(1, 0)
    fill_some(marks[7], marks[8])
    beyond_in(1, 1)
    fill_some(marks[8], marks[9])
    place_links.wait()
    rest_in(0)

    def sweep(x, blocks, weights, which, first, last):
        zero = jnp.zeros((wide, TILE), jnp.bfloat16)

        def step(g, carry):
            for j in range(WIDE_GROUP // 2):
                s = g * WIDE_GROUP + 2 * j
                x0 = jnp.concatenate([x[blocks[0, s]], zero], axis=1)
                x1 = jnp.concatenate([zero, x[blocks[0, s + 1]]], axis=1)
                both = lax.dot_general(
                    jnp.concatenate([x0, x1], axis=0),
                    weights[pl.ds(s, 2)].reshape(2 * TILE, TILE),
                    NN,
                    preferred_element_type=jnp.float32,
                )
                sums[s] = sums[links[which, s]] + both[:wide]
                sums[s + 1] = sums[links[which, s + 1]] + both[wide:]
            return carry

        lax.fori_loop(first, last, step, 0)

    def collect(which, out, first, size):
        def step(g, carry):
            for j in range(8):
                r = first + g * 8 + j
                out[r] = (sums[links[2 + which, r]] * SCALE).astype(out.dtype)
            return carry

        lax.fori_loop(0, size // 8, step, 0)

    steps = nslots // WIDE_GROUP
    hop = RB // 2
    size = hop // PARTS

    def exchange(h, k):
        def one(i, src, src_at, dst, dst_at, device):
            return remote(
                src.at[pl.ds(src_at + k * size, size)],
                dst.at[pl.ds(dst_at + k * size, size)],
                x_s.at[h, i, k],
                x_r.at[h, i, k],
                device,
            )

        return (
            one(0, part[h], (1 - side) * hop, near.at[h], 0, sibling),
            one(1, pair.at[h], 0, far_part.at[h], 0, across),
            one(2, ubuf[h], side * hop, ubuf[h], side * hop, sibling),
        )

    def give(h):
        for k in range(PARTS):
            collect(0, part[h], (1 - side) * hop + k * size, size)
            exchange(h, k)[0].start()
        collect(0, part[h], side * hop, hop)

    def swap(h, k):
        given, swapped, _ = exchange(h, k)
        given.wait_recv()
        mine = part[h][pl.ds(side * hop + k * size, size)]
        span = pl.ds(k * size, size)
        pair[h, span] = (f32(mine) + f32(near[h, span])).astype(pair.dtype)
        swapped.start()

    def settle(h, k):
        _, swapped, backward = exchange(h, k)
        swapped.wait_recv()
        span = pl.ds(k * size, size)
        total = f32(pair[h, span]) + f32(far_part[h, span])
        ubuf[h][pl.ds(side * hop + k * size, size)] = total.astype(jnp.bfloat16)
        backward.start()

    def settled(h):
        for k in range(PARTS):
            exchange(h, k)[2].wait_recv()

    def exchanged(h):
        for k in range(PARTS):
            for copy in exchange(h, k):
                copy.wait_send()

    per = RB // 4

    def write_u(h):
        for j in range(per):
            u_out[h * wide : (h + 1) * wide, j * TILE : (j + 1) * TILE] = ubuf[h][item * per + j]

    sweep(v0, cols, flipped, 0, 0, steps)
    give(0)

    def first_swaps(k, carry):
        swap(0, k)
        return carry

    lax.fori_loop(0, PARTS, first_swaps, 0)
    rest_in(1)
    sweep(v1, cols, flipped, 0, 0, steps * 3 // 4)
    settle(0, 0)
    sweep(v1, cols, flipped, 0, steps * 3 // 4, steps)
    give(1)
    for k in range(PARTS):
        swap(1, k)
        if k + 1 < PARTS:
            settle(0, k + 1)
    settled(0)
    sweep(u0, rows, tiles, 1, 0, steps)

    def piece(h, zz, yy, k):
        return wbuf[h].at[pl.ds((2 * zz + yy) * own + k * cut, cut)]

    def stage(h, i, k):
        return outbox.at[h, pl.ds(i * own + k * cut, cut)]

    box = dict(dmate=0, extra=0, dadj=1, dfar=2, cadj=3, cfar=4, mate=5, cross=6, face=7)
    posts = dict(
        dfar=((far, 1 - y), None, 0, 0, facing_dev),
        dadj=((adj, 1 - y), None, 1, 1, facing_dev),
        extra=((mate, 1 - y), None, 2, 2, mate_dev),
        dmate=((mate, 1 - y), None, 3, 3, facing_dev),
        cadj=(None, 0, 4, 4, mate_dev),
        cfar=(None, 1, 5, 5, mate_dev),
        xadj=(None, 0, 6, 6, adj_dev),
        xfar=(None, 1, 7, 6, far_dev),
        face=((z, 1 - y), 2, 8, 8, facing_dev),
        mate=((mate, y), 3, 9, 9, mate_dev),
    )
    direct = (("face", 0), ("mate", 1))

    def scatter(h, name, k):
        where, slot, si, ri, device = posts[name]
        staged = slot is not None and (name, k) not in direct
        src = stage(h, slot, k) if staged else piece(h, *where, k)
        first = box["cross" if name[0] == "x" else name] * own + k * cut
        return remote(
            src, inbox.at[h, pl.ds(first, cut)], rs_s.at[h, si, k], rs_r.at[h, ri, k], device
        )

    def scatter_first(h):
        for k in range(PIECES):
            scatter(h, "dfar", k).start()
            scatter(h, "dadj", k).start()
        scatter(h, "extra", 1).start()
        scatter(h, "dmate", 0).start()
        scatter(h, "mate", 1).start()
        scatter(h, "face", 0).start()

    def got(h, name, k):
        return f32(inbox[h, box[name] * own + k * cut : box[name] * own + (k + 1) * cut])

    def block(h, zz, yy, k):
        return f32(wbuf[h][pl.ds((2 * zz + yy) * own + k * cut, cut)])

    def put(h, i, k, value):
        outbox[h, i * own + k * cut : i * own + (k + 1) * cut] = value.astype(outbox.dtype)

    def beyond_out(h, k):
        for name, zz, i in (("far", far, 1), ("adj", adj, 0)):
            scatter(h, "d" + name, k).wait_recv()

            @pl.when(mid == 0)
            def _():
                put(h, i, k, block(h, zz, y, k) + got(h, "d" + name, k))
                scatter(h, "c" + name, k).start()

    def beyond_pass(h, k):
        @pl.when(mid == 1)
        def _():
            for name, zz, i in (("far", far, 1), ("adj", adj, 0)):
                scatter(h, "c" + name, k).wait_recv()
                both = block(h, zz, y, k) + got(h, "d" + name, k) + got(h, "c" + name, k)
                put(h, i, k, both)
                scatter(h, "x" + name, k).start()

    def near_out(h):
        scatter(h, "extra", 1).wait_recv()
        put(h, 2, 1, block(h, z, 1 - y, 1) + got(h, "extra", 1))
        scatter(h, "face", 1).start()
        scatter(h, "dmate", 0).wait_recv()
        put(h, 3, 0, block(h, mate, y, 0) + got(h, "dmate", 0))
        scatter(h, "mate", 0).start()

    def total(h):
        square = jnp.zeros((wide, TILE), jnp.float32)
        for k in range(PIECES):
            scatter(h, "mate", k).wait_recv()
            scatter(h, "face", k).wait_recv()
            scatter(h, "xadj", k).wait_recv()
            whole = block(h, z, y, k) + got(h, "mate", k) + got(h, "face", k) + got(h, "cross", k)
            for j in range(cut):
                lane = (k * cut + j) * TILE
                back[h * wide : (h + 1) * wide, lane : lane + TILE] = whole[j]
                square = square + whole[j] * whole[j]
        mine = back[h * wide : (h + 1) * wide, :]
        crossed = sum(
            lax.dot_general(lock3[:nlock], x, NT, preferred_element_type=jnp.float32)
            for x in split3(mine)
        )
        return crossed, square

    def scattered(h):
        scatter(h, "extra", 1).wait_send()
        scatter(h, "dmate", 0).wait_send()
        for k in range(PIECES):
            for name in ("dfar", "dadj", "face", "mate"):
                scatter(h, name, k).wait_send()
        for flag, names in ((0, ("cadj", "cfar")), (1, ("xadj", "xfar"))):

            @pl.when(mid == flag)
            def _():
                for k in range(PIECES):
                    for name in names:
                        scatter(h, name, k).wait_send()

    collect(1, w0, 0, nblocks)
    scatter_first(0)
    for k in range(PARTS):
        settle(1, k)
    beyond_out(0, 0)
    beyond_out(0, 1)
    settled(1)
    sweep(u1, rows, tiles, 1, 0, steps // 4)
    near_out(0)
    sweep(u1, rows, tiles, 1, steps // 4, steps // 2)
    beyond_pass(0, 0)
    sweep(u1, rows, tiles, 1, steps // 2, steps * 3 // 4)
    beyond_pass(0, 1)
    sweep(u1, rows, tiles, 1, steps * 3 // 4, steps)
    collect(1, w1, 0, nblocks)
    scatter_first(1)
    write_u(0)
    beyond_out(1, 0)
    beyond_out(1, 1)
    near_out(1)
    beyond_pass(1, 0)
    beyond_pass(1, 1)
    crossed0, square0 = total(0)
    write_u(1)
    crossed1, square1 = total(1)
    crossed = jnp.concatenate([crossed0, crossed1], axis=1)
    squares = lax.dot_general(
        jnp.ones((8, TILE), jnp.float32), jnp.concatenate([square0, square1], axis=0), NT,
        precision=HIGH, preferred_element_type=jnp.float32,
    )
    tail = jnp.concatenate(
        [
            jnp.concatenate([crossed[:half], crossed[half:]], axis=1),
            jnp.concatenate([squares, jnp.zeros_like(squares)], axis=1),
        ],
        axis=0,
    )
    pending = start_sum(plane(), tail, last_p, sp2, rp2)
    tail = end_sum(plane(), pending, last_p)
    pending = start_sum(column(), tail, last_c, sc2, rc2)
    for h in range(HALVES):
        all_sent(h)
        exchanged(h)
        scattered(h)
    tail = end_sum(column(), pending, last_c)
    stack = jnp.concatenate([tail[:half, :width], tail[:half, width:], tail[half:, :width]], axis=0)
    stack = jnp.concatenate([stack, jnp.zeros_like(stack)], axis=1).T[:width]
    proj2, backsq = stack[:, :nlock], stack[:, nlock : nlock + 1]
    folded = jnp.dot(proj2, gram, precision=HIGH) - 2.0 * proj2
    colsq = backsq + jnp.sum(proj2 * folded, axis=1, keepdims=True)
    scale = 1.0 / jnp.sqrt(jnp.maximum(colsq, 0.0) / items + 1e-06)
    gone = jnp.dot(
        jnp.concatenate(split3(proj2), axis=1), lock3[...], preferred_element_type=jnp.float32
    )
    v_out[...] = (back[...] - gone) * scale


def one_kernel_plan(v_start, locked, tile_rows, tile_cols, tile_seeds, tile_count):
    n_user, n_item = lax.axis_size("user"), lax.axis_size("item")
    shard, width = v_start.shape
    nlock = locked.shape[1]
    nslots = tile_rows.shape[1]
    nblocks = shard * n_user // TILE
    own = shard // TILE
    wide = width // HALVES
    hop = RB // 2
    bf, fl, i32 = jnp.bfloat16, jnp.float32, jnp.int32
    hbm = pl.BlockSpec(memory_space=pl.ANY)
    slab = pltpu.VMEM((nblocks, wide, TILE), bf)
    users = pltpu.VMEM((RB, wide, TILE), bf)
    trade = pltpu.VMEM((HALVES, hop, wide, TILE), bf)
    rows = nlock // 2 + 8
    u_factor, v_next = pl.pallas_call(
        functools.partial(round_kernel, float(shard * n_user * n_item)),
        name="round",
        out_shape=(
            jax.ShapeDtypeStruct((width, RB // n_item * TILE), bf),
            jax.ShapeDtypeStruct((width, shard), fl),
        ),
        in_specs=[SMEM_SPEC] + [hbm] * 5,
        out_specs=(VMEM_SPEC, VMEM_SPEC),
        scratch_shapes=[
            pltpu.SMEM((1, nslots), i32),
            pltpu.SMEM((1, nslots), i32),
            pltpu.SMEM((1, nslots), i32),
            pltpu.SMEM((8, nslots), i32),
            pltpu.VMEM((1, nslots), i32),
            pltpu.VMEM((1, nslots), i32),
            pltpu.VMEM((8, nslots), i32),
            pltpu.VMEM((width, shard), bf),
            pltpu.VMEM((3 * nlock, shard), bf),
            pltpu.VMEM((nslots, TILE, TILE), bf),
            pltpu.VMEM((nslots, TILE, TILE), bf),
            pltpu.VMEM((nslots + 1, wide, TILE), fl),
            slab, slab, users, users, trade, trade, trade, users, users, slab, slab,
            pltpu.VMEM((HALVES, 8 * own, wide, TILE), bf),
            pltpu.VMEM((HALVES, 4 * own, wide, TILE), bf),
            pltpu.VMEM((width, shard), fl),
            pltpu.VMEM((2 * n_item, rows, TILE), fl),
            pltpu.VMEM((n_user // 2, rows, TILE), fl),
            pltpu.VMEM((2 * n_item, rows, TILE), fl),
            pltpu.VMEM((n_user // 2, rows, TILE), fl),
            sems(8),
            sems(HALVES, 10, PIECES), sems(HALVES, 10, PIECES),
            sems(HALVES, 3, PARTS), sems(HALVES, 3, PARTS),
            sems(HALVES, 10, PIECES), sems(HALVES, 10, PIECES),
        ]
        + ([sems(2 * n_item - 1)] * 2 + [sems(n_user // 2 - 1)] * 2) * 2,
        compiler_params=pltpu.CompilerParams(
            collective_id=0, has_side_effects=True, vmem_limit_bytes=BIG_LIMIT
        ),
    )(tile_count, tile_rows, tile_cols, tile_seeds, v_start.T, locked.T)
    return u_factor.T, v_next.T


def fits_one_kernel(v_start, locked, tile_rows):
    return (
        v_start.shape[0] % (2 * TILE) == 0
        and v_start.shape[1] == 64
        and locked.shape[1] == 32
        and tile_rows.shape[1] % 512 == 0
        and lax.axis_size("item") == 4
        and lax.axis_size("user") == 8
    )


def on_device(v_start, locked, tile_rows, tile_cols, tile_seeds, tile_count):
    if fits_one_kernel(v_start, locked, tile_rows):
        return one_kernel_plan(v_start, locked, tile_rows, tile_cols, tile_seeds, tile_count)
    both = ("user", "item")
    lockf = locked.astype(jnp.float32)
    nlock = locked.shape[1]
    n_user, n_item = lax.axis_size("user"), lax.axis_size("item")
    slab = v_start.shape[0] * n_user
    stats = jnp.dot(
        locked.T, jnp.concatenate([v_start, locked], axis=1), preferred_element_type=jnp.float32
    )
    stats = lax.psum(stats, both)
    proj, gram = stats[:, :-nlock], stats[:, -nlock:]
    deflated = (v_start.astype(jnp.float32) - jnp.dot(lockf, proj, precision=HIGH)).astype(
        jnp.bfloat16
    )
    vslab = lax.all_gather(deflated, "user", axis=0, tiled=True)
    places = pack(tile_rows, tile_cols)
    flipped, tiles = [
        pl.pallas_call(
            functools.partial(fill_kernel, flip),
            name="fill",
            out_shape=jax.ShapeDtypeStruct((tile_seeds.shape[1], TILE, TILE), jnp.bfloat16),
            in_specs=[SMEM_SPEC],
            out_specs=VMEM_SPEC,
            compiler_params=pltpu.CompilerParams(vmem_limit_bytes=LIMIT),
        )(tile_seeds)
        for flip in (True, False)
    ]
    upart = product(True, places, tile_count, blocks_of(vslab), flipped, RB, jnp.float32)
    ublocks = lax.psum(upart, "item").astype(jnp.bfloat16)
    per = RB // n_item
    u_factor = rows_of(lax.dynamic_slice_in_dim(ublocks, lax.axis_index("item") * per, per, 0))
    wpart = product(False, places, tile_count, ublocks, tiles, slab // TILE, jnp.float32)
    back = lax.psum_scatter(rows_of(wpart), "user", scatter_dimension=0, tiled=True)
    sums = jnp.concatenate(
        [jnp.dot(lockf.T, back, precision=HIGH), jnp.sum(back * back, axis=0)[None]], axis=0
    )
    sums = lax.psum(sums, both)
    proj2, backsq = sums[:-1], sums[-1]
    rest = back - jnp.dot(lockf, proj2, precision=HIGH)
    crossed = jnp.dot(gram, proj2, precision=HIGH) - 2.0 * proj2
    colsq = jnp.maximum(backsq + jnp.sum(proj2 * crossed, axis=0), 0.0)
    v_next = rest / jnp.sqrt(colsq / (slab * n_item) + 1e-06)
    return (u_factor, v_next)


def solution(mesh):
    spec = P(("user", "item"), None)
    return jax.shard_map(
        on_device, mesh=mesh, in_specs=(spec,) * 6, out_specs=(spec, spec), check_vma=False
    )
```
